32 devices in a mesh: groups: 2 (over y), ctx: 4 (over z), tp: 2 (over x), kv: 2 (over core).
Axes of the slice: x: 2, y: 2, z: 4, core: 2. Of those that a mesh axis runs over, the one named last changes fastest.
Arguments:
- queries: bfloat16 [2048, 8192], P(('groups', 'ctx'), ('tp', 'kv')), parts along dimension 0, may hold values from -8 to 8
- key_matrix: bfloat16 [2048, 1024], P(('groups', 'ctx'), 'tp'), parts along dimension 0, may hold values from -8 to 8
- value_matrix: bfloat16 [2048, 1024], P(('groups', 'ctx'), 'tp'), parts along dimension 0, may hold values from -6 to 6
- out_grad: bfloat16 [2048, 8192], P(('groups', 'ctx'), ('tp', 'kv')), parts along dimension 0, may hold values from -6 to 6
- segments: int32 [2048], P(('groups', 'ctx')), parts along dimension 0, may hold values from 0 to 15, never falling along the last dimension, each value on 1 to 512 neighbouring positions
Outputs:
- query_grad: bfloat16 [2048, 8192], P(('groups', 'ctx'), ('tp', 'kv')), parts along dimension 0
- key_gradient: bfloat16 [2048, 1024], P(('groups', 'ctx'), 'tp'), parts along dimension 0
- value_gradient: bfloat16 [2048, 1024], P(('groups', 'ctx'), 'tp'), parts along dimension 0
The draws below stay inside these ranges and needn't reach their ends.
There are 2 independent parts, one for each index of `groups`. The reference program is written for one: setup_inputs(seed, part) draws one part's arguments, and reference() takes and returns one part's arrays. A program takes and returns all parts, laid end to end along the dimension named above; each array names one. Nothing has to cross between parts.
Inputs may be any that keep to these rules, and one draw needn't show every extreme that they name: `segments`: document numbers never fall along the sequence; each of the 16 documents has 1 or more positions and one document holds exactly half of the 1024 positions.
All inputs are finite; a program needn't handle non-finite values.
Results may differ from the reference program's by a relative error of at most 0.011.
Values may be sent and summed in bfloat16 or wider, within the bound.
A program may use at most 64 MiB of HBM per device.

```python
import math
import jax
import jax.numpy as jnp
import numpy as np
from jax import lax

QUERY_HEADS = 64
KEY_VALUE_HEADS = 8
HEAD_SIZE = 128
DOCS = 16
PACKED_LENGTH = 1024


def draw_key_matrix(key, part):
    output_rows = jnp.clip(jax.random.normal(jax.random.fold_in(key, 11), (PACKED_LENGTH, KEY_VALUE_HEADS, HEAD_SIZE), jnp.float32), -6.0, 6.0)
    return output_rows.reshape(PACKED_LENGTH, KEY_VALUE_HEADS * HEAD_SIZE).astype(jnp.bfloat16)


def draw_queries(key, part):
    output_rows = jnp.clip(jax.random.normal(jax.random.fold_in(key, 13), (PACKED_LENGTH, QUERY_HEADS, HEAD_SIZE), jnp.float32), -6.0, 6.0)
    return output_rows.reshape(PACKED_LENGTH, QUERY_HEADS * HEAD_SIZE).astype(jnp.bfloat16)


def levels(rng, shape, split, least, top_value):
    level, own = 1.0, jax.random.fold_in(rng, 6)
    for dim, blocks in split:
        draws = jnp.exp(jax.random.uniform(jax.random.fold_in(own, dim), (blocks,), jnp.float32, least / len(split), top_value / len(split)))
        level = level * jnp.repeat(draws, shape[dim] // blocks).reshape([-1 if axis == dim else 1 for axis in range(len(shape))])
    return level


def split_up(number_of, total, bound, slope):
    loads = [(1 << 20) // math.isqrt(rank ** slope) + 1 for rank in range(2, number_of + 1)]
    spare, given = total - bound - (number_of - 1), [1] * (number_of - 1)
    while spare > 0:
        movable = [i for i in range(number_of - 1) if given[i] < bound]
        whole, budget = sum([loads[i] for i in movable]), spare
        for i in movable:
            addition = min(bound - given[i], max(1, budget * loads[i] // whole), spare)
            given[i] = given[i] + addition
            spare = spare - addition
    return np.array([bound] + given)


def ragged(rng, number_of, total, reach, lean):
    if number_of == 2:
        one = jax.random.randint(rng, (), max(1, total - reach), min(reach, total - 1) + 1)
        return jnp.stack([one, total - one])
    sizes = jnp.asarray(split_up(number_of, total, reach, lean), jnp.int32)
    couples = (number_of - 1) // 2
    giver, receiver = sizes[1:1 + 2 * couples:2], sizes[2:2 + 2 * couples:2]
    margin = jnp.minimum(giver - 1, reach - receiver)
    moved = jax.random.randint(jax.random.fold_in(rng, 1), (couples,), 0, 1 << 20) % (margin + 1)
    sizes = sizes.at[1:1 + 2 * couples:2].set(giver - moved).at[2:2 + 2 * couples:2].set(receiver + moved)
    return sizes[jax.random.permutation(jax.random.fold_in(rng, 2), number_of)]


def centred(rng, shape, width, bound, pieces=(), kind=jnp.bfloat16):
    array = jax.random.normal(rng, shape, jnp.float32) * width
    if len(pieces) > 0:
        array = levels(rng, shape, pieces, -0.22, 0.18) * array
    return jnp.clip(array, min=-bound, max=bound).astype(kind)


def setup_inputs(seed: int = 0, part: int = 0) -> dict:
    seeds = jax.random.split(jax.random.key(seed), 6)
    part_splits = jax.random.split(jax.random.fold_in(seeds[5], part), 6)
    queries = draw_queries(jax.random.fold_in(jax.random.fold_in(seeds[5], part), 71), part)
    key_matrix = draw_key_matrix(jax.random.fold_in(jax.random.fold_in(seeds[5], part), 71), part)
    value_matrix = centred(part_splits[2], (PACKED_LENGTH, KEY_VALUE_HEADS * HEAD_SIZE), 1.0, 6.0, ((0, 4), (1, 2)))
    out_grad = centred(part_splits[3], (PACKED_LENGTH, QUERY_HEADS * HEAD_SIZE), 1.0, 6.0, ((0, 4), (1, 4)))
    segments = jnp.searchsorted(jnp.cumsum(ragged(part_splits[4], DOCS, PACKED_LENGTH, PACKED_LENGTH // 2, 2)), jnp.arange(PACKED_LENGTH), side="right").astype(jnp.int32)
    return {"queries": queries, "key_matrix": key_matrix, "value_matrix": value_matrix, "out_grad": out_grad, "segments": segments}


def head_backward(inputs, segments, logit_scale):
    q_head, g_head, k_head, v_head = inputs
    span_length = q_head.shape[0]
    parts_count = 8
    rows_each = span_length // parts_count
    position = jnp.arange(span_length, dtype=jnp.int32)
    query_pieces = []
    key_total = jnp.zeros((span_length, HEAD_SIZE), jnp.float32)
    value_total = jnp.zeros((span_length, HEAD_SIZE), jnp.float32)
    for piece_index in range(parts_count):
        row_first = piece_index * rows_each
        row_end = row_first + rows_each
        q_rows = q_head[row_first:row_end]
        g_rows = g_head[row_first:row_end]
        k_rows = k_head[:row_end]
        v_rows = v_head[:row_end]
        allowed = (segments[row_first:row_end, None] == segments[None, :row_end]) & (position[None, :row_end] <= position[row_first:row_end, None])
        logits = jnp.dot(q_rows, k_rows.T, preferred_element_type=jnp.float32) * logit_scale
        masked_logits = jnp.where(allowed, logits, -jnp.inf)
        row_peak = jnp.max(masked_logits, axis=1, keepdims=True)
        totals = jnp.sum(jnp.where(allowed, jnp.exp(logits - row_peak), 0.0), axis=1, keepdims=True)
        log_total = row_peak + jnp.log(totals)
        probs = jnp.where(allowed, jnp.exp(logits - log_total), 0.0)
        dprobs = jnp.dot(g_rows, v_rows.T, preferred_element_type=jnp.float32)
        deltas = jnp.sum(probs * dprobs, axis=1, keepdims=True)
        dlogits = probs * (dprobs - deltas)
        probs_low = probs.astype(jnp.bfloat16)
        dlogits_low = dlogits.astype(jnp.bfloat16)
        query_pieces.append(jnp.dot(dlogits_low, k_rows, preferred_element_type=jnp.float32) * logit_scale)
        key_piece = jnp.dot(dlogits_low.T, q_rows, preferred_element_type=jnp.float32)
        value_piece = jnp.dot(probs_low.T, g_rows, preferred_element_type=jnp.float32)
        key_total = key_total + jnp.pad(key_piece, ((0, span_length - row_end), (0, 0)))
        value_total = value_total + jnp.pad(value_piece, ((0, span_length - row_end), (0, 0)))
    return jnp.concatenate(query_pieces, axis=0), key_total, value_total


def reference(queries, key_matrix, value_matrix, out_grad, segments):
    span_length = queries.shape[0]
    group_width = QUERY_HEADS // KEY_VALUE_HEADS
    logit_scale = HEAD_SIZE ** -0.5
    q_heads = queries.reshape(span_length, QUERY_HEADS, HEAD_SIZE).transpose(1, 0, 2)
    g_heads = out_grad.reshape(span_length, QUERY_HEADS, HEAD_SIZE).transpose(1, 0, 2)
    key_head_list = jnp.repeat(key_matrix.reshape(span_length, KEY_VALUE_HEADS, HEAD_SIZE).transpose(1, 0, 2), group_width, axis=0)
    value_head_list = jnp.repeat(value_matrix.reshape(span_length, KEY_VALUE_HEADS, HEAD_SIZE).transpose(1, 0, 2), group_width, axis=0)

    def one_head(inputs):
        return head_backward(inputs, segments, logit_scale)

    query_parts, key_portions, value_portions = lax.map(one_head, (q_heads, g_heads, key_head_list, value_head_list))
    query_grad = query_parts.transpose(1, 0, 2).reshape(span_length, QUERY_HEADS * HEAD_SIZE).astype(jnp.bfloat16)
    key_total_sum = jnp.sum(key_portions.reshape(KEY_VALUE_HEADS, group_width, span_length, HEAD_SIZE), axis=1) * logit_scale
    value_total_sum = jnp.sum(value_portions.reshape(KEY_VALUE_HEADS, group_width, span_length, HEAD_SIZE), axis=1)
    key_gradient = key_total_sum.transpose(1, 0, 2).reshape(span_length, KEY_VALUE_HEADS * HEAD_SIZE).astype(jnp.bfloat16)
    value_gradient = value_total_sum.transpose(1, 0, 2).reshape(span_length, KEY_VALUE_HEADS * HEAD_SIZE).astype(jnp.bfloat16)
    return query_grad, key_gradient, value_gradient
```

```python
import functools
import jax
import jax.numpy as jnp
from jax import lax
from jax.experimental import pallas as pl
from jax.experimental.pallas import tpu as pltpu
from jax.sharding import PartitionSpec as P

QUERY_HEADS = 64
KEY_VALUE_HEADS = 8
HEAD_SIZE = 128
HALF = 128
CHUNK = 32
LOG2E = 1.4426950408889634
NEG = -1e30
MESH = pl.DeviceIdType.MESH
NT = (((1,), (1,)), ((), ()))


def kernel(
    n, reach, rows, per_kv, kv_count, shared,
    q_hbm, k_hbm, v_hbm, g_hbm, seg_hbm,
    dqv, fin, other,
    qv, gv, ev, dpv, stats, fac, deltas, pv, dsv, win, segwin, bias, kt, acc, sendb, ret, pfin,
    seg_sem, load_sem, own_sem, seg_send, seg_recv, send_sem, recv_sem, back_send, back_recv,
    pair_send, pair_recv,
):
    rank = lax.axis_index("ctx")
    kv = lax.axis_index("kv")
    up = lax.rem(rank + 1, n)
    down = lax.rem(rank + n - 1, n)
    mate = 1 - kv
    scale = HEAD_SIZE ** -0.5
    width = reach * rows + HALF
    halves = rows // HALF
    pairs = per_kv // 2
    first = 0 if shared else kv * kv_count

    def cols(base, g):
        if shared:
            return pl.ds(g * HEAD_SIZE, HEAD_SIZE)
        return pl.ds(pl.multiple_of((base + g) * HEAD_SIZE, HEAD_SIZE), HEAD_SIZE)

    def slot(d):
        return pl.ds((reach - d) * rows, rows)

    seg_load = pltpu.make_async_copy(seg_hbm, segwin.at[0], seg_sem.at[0])

    def own(t, g):
        ref = k_hbm if t == 0 else v_hbm
        return pltpu.make_async_copy(
            ref.at[:, cols(first, g)], win.at[t, g, slot(0)], own_sem.at[t, g]
        )

    def load(t, head):
        ref, to = ((q_hbm, qv), (g_hbm, gv))[t]
        return pltpu.make_async_copy(
            ref.at[:, pl.ds(head * HEAD_SIZE, HEAD_SIZE)], to.at[head], load_sem.at[t, head]
        )

    def group_loads(g):
        heads = range(g * per_kv, (g + 1) * per_kv)
        return [own(t, g) for t in range(2)] + [load(t, i) for i in heads for t in range(2)]

    def forward(t, g, d):
        ref = k_hbm if t == 0 else v_hbm
        src = ref.at[:, cols(first, g)] if d == 0 else win.at[t, g, slot(d)]
        return pltpu.make_async_remote_copy(
            src_ref=src,
            dst_ref=win.at[t, g, slot(d + 1)],
            send_sem=send_sem.at[t, g, d],
            recv_sem=recv_sem.at[t, g, d + 1],
            device_id={"ctx": up},
            device_id_type=MESH,
        )

    def forward_seg(d):
        return pltpu.make_async_remote_copy(
            src_ref=seg_hbm if d == 0 else segwin.at[d],
            dst_ref=segwin.at[d + 1],
            send_sem=seg_send.at[d],
            recv_sem=seg_recv.at[d + 1],
            device_id={"ctx": up},
            device_id_type=MESH,
        )

    def pieces(kinds):
        return [(t, r) for t in kinds for r in range(halves)]

    def some(r):
        return pl.ds(r * HALF, HALF)

    def back(g, d, t, r):
        return pltpu.make_async_remote_copy(
            src_ref=sendb.at[g, d - 1, t, some(r)],
            dst_ref=ret.at[g, d - 1, t, some(r)],
            send_sem=back_send.at[g, d - 1, t, r],
            recv_sem=back_recv.at[g, d - 1, t, r],
            device_id={"ctx": down},
            device_id_type=MESH,
        )

    def owed(g, d, t, r):
        return acc[g, t, pl.ds((reach - d) * rows + r * HALF, HALF), :]

    def to_mate(g, t, r):
        return pltpu.make_async_remote_copy(
            src_ref=fin.at[g, t, some(r)],
            dst_ref=pfin.at[g, t, some(r)],
            send_sem=pair_send.at[g, t, r],
            recv_sem=pair_recv.at[g, t, r],
            device_id={"kv": mate},
            device_id_type=MESH,
        )

    has_up = rank < n - 1

    seg_load.start()
    for g in range(kv_count):
        for copy in group_loads(g):
            copy.start()

    barrier = pltpu.get_barrier_semaphore()
    pl.semaphore_signal(barrier, inc=1, device_id={"kv": mate}, device_id_type=MESH)

    @pl.when(has_up)
    def _():
        pl.semaphore_signal(barrier, inc=1, device_id={"ctx": up}, device_id_type=MESH)

    @pl.when(rank > 0)
    def _():
        pl.semaphore_signal(barrier, inc=1, device_id={"ctx": down}, device_id_type=MESH)

    expected = 1 + jnp.where(has_up, 1, 0) + jnp.where(rank > 0, 1, 0)
    pl.semaphore_wait(barrier, expected)

    @pl.when(has_up)
    def _():
        forward_seg(0).start()
        forward(0, 0, 0).start()
        forward(1, 0, 0).start()

    units = pairs * halves

    def pass_on_seg():
        for d in range(1, reach + 1):
            @pl.when(rank >= d)
            def _(d=d):
                forward_seg(d - 1).wait_recv()

            if d < reach:
                @pl.when((rank >= d) & has_up)
                def _(d=d):
                    forward_seg(d).start()

    def receive(g, d, t):
        @pl.when(rank >= d)
        def _():
            forward(t, g, d - 1).wait_recv()

        if d < reach:
            @pl.when((rank >= d) & has_up)
            def _():
                forward(t, g, d).start()

    def send_own(g):
        @pl.when(has_up)
        def _():
            for t in range(2):
                forward(t, g, 0).start()

    def part(d, h):
        start = (reach - d) * rows - h * HALF
        return max(start, 0), min(start + rows, width)

    def make_bias(d):
        column = jnp.broadcast_to(segwin[d].astype(jnp.float32), (HALF, rows)).T
        for h in range(halves):
            lo, hi = part(d, h)
            begin = lo + h * HALF - (reach - d) * rows
            seg_q = segwin[0, :, h * HALF:(h + 1) * HALF].astype(jnp.float32)
            keep = column[begin:begin + hi - lo] == seg_q
            if d == 0:
                key_at = lax.broadcasted_iota(jnp.int32, (hi - lo, HALF), 0)
                query_at = lax.broadcasted_iota(jnp.int32, (hi - lo, HALF), 1)
                keep = keep & (key_at + begin <= query_at + h * HALF)
            bias[h, lo:hi, :] = jnp.where(keep, 0.0, NEG)

    def pair(ref, g, h, p):
        head = g * per_kv + 2 * p
        return ref[head:head + 2, h * HALF:(h + 1) * HALF, :].reshape(2 * HALF, HEAD_SIZE)

    def stack(ref, g, h):
        return ref[g * per_kv:(g + 1) * per_kv, h * HALF:(h + 1) * HALF, :].reshape(
            per_kv * HALF, HEAD_SIZE
        )

    def products(g, d, p, h):
        lo, hi = part(d, h)
        span = slice(lo + h * HALF, hi + h * HALF)
        s = lax.dot_general(
            win[0, g, span, :], pair(qv, g, h, p), NT, preferred_element_type=jnp.float32
        )
        b = bias[h, lo:hi, :]
        s = s + jnp.concatenate([b, b], axis=1)
        ev[g, p, h, lo:hi, :] = s
        u = p * halves + h
        stats[g, d, 0, u:u + 1, :] = jnp.max(s, axis=0, keepdims=True)
        dpv[g, p, h, lo:hi, :] = lax.dot_general(
            win[1, g, span, :], pair(gv, g, h, p), NT, preferred_element_type=jnp.float32
        )

    def exponentials(g, d, p, h):
        lo, hi = part(d, h)
        u = p * halves + h
        peak = stats[g, d, 0, u:u + 1, :]
        total = jnp.zeros((8, 2 * HALF), jnp.float32)
        weighted = jnp.zeros((8, 2 * HALF), jnp.float32)
        for c in range(lo, hi, CHUNK):
            at = slice(c, c + CHUNK)
            e = jnp.exp2((ev[g, p, h, at, :] - peak) * (scale * LOG2E))
            ev[g, p, h, at, :] = e
            total = total + jnp.sum(e.reshape(-1, 8, 2 * HALF), axis=0)
            weighted = weighted + jnp.sum(
                (e * dpv[g, p, h, at, :]).reshape(-1, 8, 2 * HALF), axis=0
            )
        stats[g, d, 1, u:u + 1, :] = jnp.sum(total, axis=0, keepdims=True)
        stats[g, d, 2, u:u + 1, :] = jnp.sum(weighted, axis=0, keepdims=True)

    def look(g, d):
        @pl.when(rank >= d)
        def _():
            todo = [(p, h) for p in range(pairs) for h in range(halves)]
            products(g, d, *todo[0])
            for i, at in enumerate(todo):
                if i + 1 < len(todo):
                    products(g, d, *todo[i + 1])
                exponentials(g, d, *at)

    def combine(g):
        peak = stats[g, 0, 0]
        for d in range(1, reach + 1):
            peak = jnp.maximum(peak, stats[g, d, 0])
        total = jnp.zeros((units, 2 * HALF), jnp.float32)
        weighted = jnp.zeros((units, 2 * HALF), jnp.float32)
        for d in range(reach + 1):
            f = jnp.exp2((stats[g, d, 0] - peak) * (scale * LOG2E))
            total = total + f * stats[g, d, 1]
            weighted = weighted + f * stats[g, d, 2]
        inv = 1.0 / total
        for d in range(reach + 1):
            f = jnp.exp2((stats[g, d, 0] - peak) * (scale * LOG2E))
            fac[d] = f * inv
        deltas[...] = weighted * inv

    def scores(g, d, h):
        lo, hi = part(d, h)
        for p in range(pairs):
            u = p * halves + h
            f = fac[d, u:u + 1, :]
            delta = deltas[u:u + 1, :]
            there = slice(p * 2 * HALF, (p + 1) * 2 * HALF)
            for c in range(lo, hi, CHUNK):
                at = slice(c, c + CHUNK)
                pn = ev[g, p, h, at, :] * f
                dsv[h, at, there] = (pn * (dpv[g, p, h, at, :] - delta)).astype(jnp.bfloat16)
                pv[h, at, there] = pn.astype(jnp.bfloat16)

    def gradients(g, d, h, add):
        lo, hi = part(d, h)
        span = slice(lo + h * HALF, hi + h * HALF)
        for t, low, ref in ((0, dsv, qv), (1, pv, gv)):
            out = jnp.dot(
                low[h, lo:hi, :], stack(ref, g, h), preferred_element_type=jnp.float32
            )
            if add:
                acc[g, t, span, :] += out
            else:
                acc[g, t, span, :] = out

    def settle(g, d):
        @pl.when(rank >= d)
        def _():
            order = list(range(halves)) if d > 0 else list(range(halves - 1, -1, -1))
            kt[g, :, slot(d)] = win[0, g, slot(d), :].T
            for h in order:
                scores(g, d, h)
            for i, h in enumerate(order):
                gradients(g, d, h, i > 0)

    def query_gradients(g):
        for h in range(halves):
            dqt = jnp.dot(
                kt[g, :, h * HALF:h * HALF + width], dsv[h], preferred_element_type=jnp.float32
            )
            dq = (dqt * scale).T.astype(jnp.bfloat16)
            for i in range(per_kv):
                at = (g * per_kv + i) * HEAD_SIZE
                dqv[h * HALF:(h + 1) * HALF, at:at + HEAD_SIZE] = dq[i * HALF:(i + 1) * HALF]

    def send_first(g, d):
        @pl.when((rank >= d) if d == reach else ((rank >= d) & jnp.logical_not(has_up)))
        def _():
            for t, r in pieces((0, 1)):
                sendb[g, d - 1, t, some(r), :] = owed(g, d, t, r).astype(jnp.bfloat16)
                back(g, d, t, r).start()

    def send_rest(g, kinds):
        for d in range(reach - 1, 0, -1):
            @pl.when(has_up & (rank >= d))
            def _(d=d):
                for t, r in pieces(kinds):
                    back(g, d + 1, t, r).wait_recv()
                    sendb[g, d - 1, t, some(r), :] = (
                        owed(g, d, t, r) + ret[g, d, t, some(r), :].astype(jnp.float32)
                    ).astype(jnp.bfloat16)
                    back(g, d, t, r).start()

    def finish(g):
        for t, r in pieces((0, 1)):
            @pl.when(has_up)
            def _(t=t, r=r):
                back(g, 1, t, r).wait_recv()
                acc[g, t, pl.ds(reach * rows + r * HALF, HALF), :] += (
                    ret[g, 0, t, some(r), :].astype(jnp.float32)
                )

            factor = scale if t == 0 else 1.0
            fin[g, t, some(r), :] = (owed(g, 0, t, r) * factor).astype(jnp.bfloat16)
            to_mate(g, t, r).start()

    for d in range(1, reach + 1):
        @pl.when(rank < d)
        def _(d=d):
            for g in range(kv_count):
                kt[g, :, slot(d)] = jnp.zeros((HEAD_SIZE, rows), jnp.bfloat16)
                stats[g, d, 0] = jnp.full((units, 2 * HALF), NEG, jnp.float32)
                stats[g, d, 1] = jnp.zeros((units, 2 * HALF), jnp.float32)
                stats[g, d, 2] = jnp.zeros((units, 2 * HALF), jnp.float32)
            for h in range(halves):
                lo, hi = part(d, h)
                dsv[h, lo:hi, :] = jnp.zeros((hi - lo, pairs * 2 * HALF), jnp.bfloat16)

    last = kv_count - 1
    seg_load.wait()
    make_bias(0)
    for copy in group_loads(0):
        copy.wait()
    look(0, 0)
    pass_on_seg()
    for d in range(1, reach):
        for t in range(2):
            receive(0, d, t)
    if last > 0:
        send_own(1)
    for d in range(1, reach + 1):
        @pl.when(rank >= d)
        def _(d=d):
            make_bias(d)
    for d in range(1, reach):
        look(0, d)
    for g in range(kv_count):
        if g + 1 < kv_count:
            for copy in group_loads(g + 1):
                copy.wait()
            look(g + 1, 0)
        for t in range(2):
            receive(g, reach, t)
        look(g, reach)
        combine(g)
        for d in range(reach, 0, -1):
            settle(g, d)
            send_first(g, d)
        if g + 1 < kv_count:
            for d in range(1, reach):
                for t in range(2):
                    receive(g + 1, d, t)
            if g + 2 < kv_count:
                send_own(g + 2)
        settle(g, 0)
        query_gradients(g)
        if g + 1 < kv_count:
            for d in range(1, reach):
                look(g + 1, d)
        send_rest(g, (0, 1))
    for g in range(kv_count):
        finish(g)

    for g in range(kv_count):
        for t in range(2):
            for r in range(halves):
                to_mate(g, t, r).wait()
            if shared:
                other[g, t] = (
                    fin[g, t].astype(jnp.float32) + pfin[g, t].astype(jnp.float32)
                ).astype(jnp.bfloat16)
            else:
                other[g, t] = pfin[g, t]
    for d in range(reach):
        @pl.when(has_up & (rank >= d))
        def _(d=d):
            forward_seg(d).wait_send()
            for g in range(kv_count):
                for t in range(2):
                    forward(t, g, d).wait_send()
    for d in range(1, reach + 1):
        @pl.when(rank >= d)
        def _(d=d):
            for g in range(kv_count):
                for t, r in pieces((0, 1)):
                    back(g, d, t, r).wait_send()


def place(kv_count, shared, dqv, fin, other, dq_hbm, dk_hbm, dv_hbm, sem):
    kv = lax.axis_index("kv")
    copies = [pltpu.make_async_copy(dqv, dq_hbm, sem.at[0])]
    parts = [(other, 0)] if shared else [(fin, kv * kv_count), (other, (1 - kv) * kv_count)]
    for source, base in parts:
        for g in range(kv_count):
            start = g * HEAD_SIZE
            if not shared:
                start = pl.multiple_of((base + g) * HEAD_SIZE, HEAD_SIZE)
            for t, ref in ((0, dk_hbm), (1, dv_hbm)):
                copies.append(
                    pltpu.make_async_copy(
                        source.at[g, t], ref.at[:, pl.ds(start, HEAD_SIZE)], sem.at[len(copies)]
                    )
                )
    for copy in copies:
        copy.start()
    for copy in copies:
        copy.wait()


def shards(queries, key_matrix, value_matrix, out_grad, segments):
    n = lax.axis_size("ctx")
    rows = queries.shape[0]
    head_count = queries.shape[1] // HEAD_SIZE
    group_width = QUERY_HEADS // KEY_VALUE_HEADS
    kv_count = max(head_count // group_width, 1)
    per_kv = head_count // kv_count
    kv_here = key_matrix.shape[1] // HEAD_SIZE
    shared = kv_here < kv_count * lax.axis_size("kv")
    reach = n // 2
    window = (reach + 1) * rows
    width = reach * rows + HALF
    halves = rows // HALF
    pairs = per_kv // 2
    bf16, f32 = jnp.bfloat16, jnp.float32
    dma = pltpu.SemaphoreType.DMA
    anywhere = pl.BlockSpec(memory_space=pltpu.HBM)
    inner = pltpu.VMEM
    dqv, fin, other = pl.pallas_call(
        functools.partial(kernel, n, reach, rows, per_kv, kv_count, shared),
        out_shape=(
            inner(queries.shape, bf16),
            inner((kv_count, 2, rows, HEAD_SIZE), bf16),
            inner((kv_count, 2, rows, HEAD_SIZE), bf16),
        ),
        in_specs=[anywhere] * 5,
        out_specs=(pl.BlockSpec(memory_space=pltpu.VMEM),) * 3,
        scratch_shapes=[
            pltpu.VMEM((head_count, rows, HEAD_SIZE), bf16),
            pltpu.VMEM((head_count, rows, HEAD_SIZE), bf16),
            pltpu.VMEM((kv_count, pairs, halves, width, 2 * HALF), f32),
            pltpu.VMEM((kv_count, pairs, halves, width, 2 * HALF), f32),
            pltpu.VMEM((kv_count, reach + 1, 3, pairs * halves, 2 * HALF), f32),
            pltpu.VMEM((reach + 1, pairs * halves, 2 * HALF), f32),
            pltpu.VMEM((pairs * halves, 2 * HALF), f32),
            pltpu.VMEM((halves, width, pairs * 2 * HALF), bf16),
            pltpu.VMEM((halves, width, pairs * 2 * HALF), bf16),
            pltpu.VMEM((2, kv_count, window, HEAD_SIZE), bf16),
            pltpu.VMEM((reach + 1, 1, rows), jnp.int32),
            pltpu.VMEM((halves, width, HALF), f32),
            pltpu.VMEM((kv_count, HEAD_SIZE, window), bf16),
            pltpu.VMEM((kv_count, 2, window, HEAD_SIZE), f32),
            pltpu.VMEM((kv_count, reach, 2, rows, HEAD_SIZE), bf16),
            pltpu.VMEM((kv_count, reach, 2, rows, HEAD_SIZE), bf16),
            pltpu.VMEM((kv_count, 2, rows, HEAD_SIZE), bf16),
            dma((1,)),
            dma((2, head_count)),
            dma((2, kv_count)),
            dma((reach + 1,)),
            dma((reach + 1,)),
            dma((2, kv_count, reach + 1)),
            dma((2, kv_count, reach + 1)),
            dma((kv_count, reach, 2, halves)),
            dma((kv_count, reach, 2, halves)),
            dma((kv_count, 2, halves)),
            dma((kv_count, 2, halves)),
        ],
        compiler_params=pltpu.CompilerParams(
            collective_id=0, has_side_effects=True, vmem_limit_bytes=56 * 1024 * 1024
        ),
    )(queries, key_matrix, value_matrix, out_grad, segments.reshape(1, rows))
    return pl.pallas_call(
        functools.partial(place, kv_count, shared),
        out_shape=(
            jax.ShapeDtypeStruct(queries.shape, bf16),
            jax.ShapeDtypeStruct(key_matrix.shape, bf16),
            jax.ShapeDtypeStruct(value_matrix.shape, bf16),
        ),
        in_specs=[pl.BlockSpec(memory_space=pltpu.VMEM)] * 3,
        out_specs=(anywhere,) * 3,
        scratch_shapes=[dma((1 + 4 * kv_count,))],
        compiler_params=pltpu.CompilerParams(vmem_limit_bytes=4 * 1024 * 1024),
    )(dqv, fin, other)


def solution(mesh):
    return jax.shard_map(
        shards,
        mesh=mesh,
        in_specs=(
            P(("groups", "ctx"), ("tp", "kv")),
            P(("groups", "ctx"), "tp"),
            P(("groups", "ctx"), "tp"),
            P(("groups", "ctx"), ("tp", "kv")),
            P(("groups", "ctx")),
        ),
        out_specs=(
            P(("groups", "ctx"), ("tp", "kv")),
            P(("groups", "ctx"), "tp"),
            P(("groups", "ctx"), "tp"),
        ),
        check_vma=False,
    )
```

```python
import functools
import jax
import jax.numpy as jnp
from jax import lax
from jax.experimental import pallas as pl
from jax.experimental.pallas import tpu as pltpu
from jax.sharding import PartitionSpec as P

QUERY_HEADS = 64
KEY_VALUE_HEADS = 8
HEAD_SIZE = 128
HALF = 128
CHUNK = 32
LOG2E = 1.4426950408889634
NEG = -1e30
MESH = pl.DeviceIdType.MESH
NT = (((1,), (1,)), ((), ()))


def kernel(
    n, reach, rows, per_kv, kv_count, shared,
    q_hbm, k_hbm, v_hbm, g_hbm, seg_hbm,
    dqv, fin, other,
    qv, gv, ev, dpv, stats, fac, deltas, pv, dsv, win, segwin, bias, kt, acc, sendb, ret, pfin,
    seg_sem, load_sem, own_sem, seg_send, seg_recv, send_sem, recv_sem, back_send, back_recv,
    pair_send, pair_recv,
):
    rank = lax.axis_index("ctx")
    kv = lax.axis_index("kv")
    up = lax.rem(rank + 1, n)
    down = lax.rem(rank + n - 1, n)
    mate = 1 - kv
    scale = HEAD_SIZE ** -0.5
    width = reach * rows + HALF
    halves = rows // HALF
    pairs = per_kv // 2
    first = 0 if shared else kv * kv_count

    def cols(base, g):
        if shared:
            return pl.ds(g * HEAD_SIZE, HEAD_SIZE)
        return pl.ds(pl.multiple_of((base + g) * HEAD_SIZE, HEAD_SIZE), HEAD_SIZE)

    def slot(d):
        return pl.ds((reach - d) * rows, rows)

    seg_load = pltpu.make_async_copy(seg_hbm, segwin.at[0], seg_sem.at[0])

    def own(t, g):
        ref = k_hbm if t == 0 else v_hbm
        return pltpu.make_async_copy(
            ref.at[:, cols(first, g)], win.at[t, g, slot(0)], own_sem.at[t, g]
        )

    def load(t, head):
        ref, to = ((q_hbm, qv), (g_hbm, gv))[t]
        return pltpu.make_async_copy(
            ref.at[:, pl.ds(head * HEAD_SIZE, HEAD_SIZE)], to.at[head], load_sem.at[t, head]
        )

    def group_loads(g, t):
        return [own(t, g)] + [load(t, i) for i in range(g * per_kv, (g + 1) * per_kv)]

    def forward(t, g, d):
        ref = k_hbm if t == 0 else v_hbm
        src = ref.at[:, cols(first, g)] if d == 0 else win.at[t, g, slot(d)]
        return pltpu.make_async_remote_copy(
            src_ref=src,
            dst_ref=win.at[t, g, slot(d + 1)],
            send_sem=send_sem.at[t, g, d],
            recv_sem=recv_sem.at[t, g, d + 1],
            device_id={"ctx": up},
            device_id_type=MESH,
        )

    def forward_seg(d):
        return pltpu.make_async_remote_copy(
            src_ref=seg_hbm if d == 0 else segwin.at[d],
            dst_ref=segwin.at[d + 1],
            send_sem=seg_send.at[d],
            recv_sem=seg_recv.at[d + 1],
            device_id={"ctx": up},
            device_id_type=MESH,
        )

    def pieces(kinds):
        return [(t, r) for t in kinds for r in range(halves)]

    def some(r):
        return pl.ds(r * HALF, HALF)

    def back(g, d, t, r):
        return pltpu.make_async_remote_copy(
            src_ref=sendb.at[g, d - 1, t, some(r)],
            dst_ref=ret.at[g, d - 1, t, some(r)],
            send_sem=back_send.at[g, d - 1, t, r],
            recv_sem=back_recv.at[g, d - 1, t, r],
            device_id={"ctx": down},
            device_id_type=MESH,
        )

    def owed(g, d, t, r):
        return acc[g, t, pl.ds((reach - d) * rows + r * HALF, HALF), :]

    def to_mate(g, t, r):
        return pltpu.make_async_remote_copy(
            src_ref=fin.at[g, t, some(r)],
            dst_ref=pfin.at[g, t, some(r)],
            send_sem=pair_send.at[g, t, r],
            recv_sem=pair_recv.at[g, t, r],
            device_id={"kv": mate},
            device_id_type=MESH,
        )

    has_up = rank < n - 1

    seg_load.start()
    for g in range(kv_count):
        for t in range(2):
            for copy in group_loads(g, t):
                copy.start()

    barrier = pltpu.get_barrier_semaphore()
    pl.semaphore_signal(barrier, inc=1, device_id={"kv": mate}, device_id_type=MESH)

    @pl.when(has_up)
    def _():
        pl.semaphore_signal(barrier, inc=1, device_id={"ctx": up}, device_id_type=MESH)

    @pl.when(rank > 0)
    def _():
        pl.semaphore_signal(barrier, inc=1, device_id={"ctx": down}, device_id_type=MESH)

    expected = 1 + jnp.where(has_up, 1, 0) + jnp.where(rank > 0, 1, 0)
    pl.semaphore_wait(barrier, expected)

    @pl.when(has_up)
    def _():
        forward_seg(0).start()
        forward(0, 0, 0).start()

    units = pairs * halves

    def receive_seg(d):
        @pl.when(rank >= d)
        def _():
            forward_seg(d - 1).wait_recv()

        if d < reach:
            @pl.when((rank >= d) & has_up)
            def _():
                forward_seg(d).start()

    def receive(g, d, t):
        @pl.when(rank >= d)
        def _():
            forward(t, g, d - 1).wait_recv()

        if d < reach:
            @pl.when((rank >= d) & has_up)
            def _():
                forward(t, g, d).start()

    def send_own(g, t):
        @pl.when(has_up)
        def _():
            forward(t, g, 0).start()

    def part(d, h):
        start = (reach - d) * rows - h * HALF
        return max(start, 0), min(start + rows, width)

    def make_bias(d):
        column = jnp.broadcast_to(segwin[d].astype(jnp.float32), (HALF, rows)).T
        for h in range(halves):
            lo, hi = part(d, h)
            begin = lo + h * HALF - (reach - d) * rows
            seg_q = segwin[0, :, h * HALF:(h + 1) * HALF].astype(jnp.float32)
            keep = column[begin:begin + hi - lo] == seg_q
            if d == 0:
                key_at = lax.broadcasted_iota(jnp.int32, (hi - lo, HALF), 0)
                query_at = lax.broadcasted_iota(jnp.int32, (hi - lo, HALF), 1)
                keep = keep & (key_at + begin <= query_at + h * HALF)
            bias[h, lo:hi, :] = jnp.where(keep, 0.0, NEG)

    def biased(d):
        @pl.when(rank >= d)
        def _():
            make_bias(d)

    def pair(ref, g, h, p):
        head = g * per_kv + 2 * p
        return ref[head:head + 2, h * HALF:(h + 1) * HALF, :].reshape(2 * HALF, HEAD_SIZE)

    def stack(ref, g, h):
        return ref[g * per_kv:(g + 1) * per_kv, h * HALF:(h + 1) * HALF, :].reshape(
            per_kv * HALF, HEAD_SIZE
        )

    def key_products(g, d, p, h):
        lo, hi = part(d, h)
        span = slice(lo + h * HALF, hi + h * HALF)
        s = lax.dot_general(
            win[0, g, span, :], pair(qv, g, h, p), NT, preferred_element_type=jnp.float32
        )
        b = bias[h, lo:hi, :]
        s = s + jnp.concatenate([b, b], axis=1)
        ev[g, p, h, lo:hi, :] = s
        u = p * halves + h
        stats[g, d, 0, u:u + 1, :] = jnp.max(s, axis=0, keepdims=True)

    def exponentials(g, d, p, h):
        lo, hi = part(d, h)
        u = p * halves + h
        peak = stats[g, d, 0, u:u + 1, :]
        total = jnp.zeros((8, 2 * HALF), jnp.float32)
        for c in range(lo, hi, CHUNK):
            at = slice(c, c + CHUNK)
            e = jnp.exp2((ev[g, p, h, at, :] - peak) * (scale * LOG2E))
            ev[g, p, h, at, :] = e
            total = total + jnp.sum(e.reshape(-1, 8, 2 * HALF), axis=0)
        stats[g, d, 1, u:u + 1, :] = jnp.sum(total, axis=0, keepdims=True)

    def value_products(g, d, p, h):
        lo, hi = part(d, h)
        span = slice(lo + h * HALF, hi + h * HALF)
        u = p * halves + h
        dp = lax.dot_general(
            win[1, g, span, :], pair(gv, g, h, p), NT, preferred_element_type=jnp.float32
        )
        dpv[g, p, h, lo:hi, :] = dp
        stats[g, d, 2, u:u + 1, :] = jnp.sum(ev[g, p, h, lo:hi, :] * dp, axis=0, keepdims=True)

    todo = [(p, h) for p in range(pairs) for h in range(halves)]

    def look_keys(g, d):
        @pl.when(rank >= d)
        def _():
            key_products(g, d, *todo[0])
            for i, at in enumerate(todo):
                if i + 1 < len(todo):
                    key_products(g, d, *todo[i + 1])
                exponentials(g, d, *at)

    def look_values(g, d):
        @pl.when(rank >= d)
        def _():
            for at in todo:
                value_products(g, d, *at)

    def combine_keys(g):
        peak = stats[g, 0, 0]
        for d in range(1, reach + 1):
            peak = jnp.maximum(peak, stats[g, d, 0])
        total = jnp.zeros((units, 2 * HALF), jnp.float32)
        for d in range(reach + 1):
            f = jnp.exp2((stats[g, d, 0] - peak) * (scale * LOG2E))
            fac[g, d] = f
            total = total + f * stats[g, d, 1]
        inv = 1.0 / total
        for d in range(reach + 1):
            fac[g, d] = fac[g, d] * inv

    def combine_values(g):
        weighted = jnp.zeros((units, 2 * HALF), jnp.float32)
        for d in range(reach + 1):
            weighted = weighted + fac[g, d] * stats[g, d, 2]
        deltas[g] = weighted

    def settle(g, d, t):
        @pl.when(rank >= d)
        def _():
            order = list(range(halves)) if d > 0 else list(range(halves - 1, -1, -1))
            for i, h in enumerate(order):
                lo, hi = part(d, h)
                for p in range(pairs):
                    u = p * halves + h
                    f = fac[g, d, u:u + 1, :]
                    there = slice(p * 2 * HALF, (p + 1) * 2 * HALF)
                    for c in range(lo, hi, CHUNK):
                        at = slice(c, c + CHUNK)
                        pn = ev[g, p, h, at, :] * f
                        if t == 0:
                            delta = deltas[g, u:u + 1, :]
                            dsv[h, at, there] = (
                                pn * (dpv[g, p, h, at, :] - delta)
                            ).astype(jnp.bfloat16)
                        else:
                            pv[h, at, there] = pn.astype(jnp.bfloat16)
            for i, h in enumerate(order):
                lo, hi = part(d, h)
                span = slice(lo + h * HALF, hi + h * HALF)
                low, ref = ((dsv, qv), (pv, gv))[t]
                out = jnp.dot(
                    low[h, lo:hi, :], stack(ref, g, h), preferred_element_type=jnp.float32
                )
                if i > 0:
                    acc[g, t, span, :] += out
                else:
                    acc[g, t, span, :] = out

    def query_gradients(g):
        for d in range(reach + 1):
            @pl.when(rank >= d)
            def _(d=d):
                kt[g, :, slot(d)] = win[0, g, slot(d), :].T
        for h in range(halves):
            dqt = jnp.dot(
                kt[g, :, h * HALF:h * HALF + width], dsv[h], preferred_element_type=jnp.float32
            )
            dq = (dqt * scale).T.astype(jnp.bfloat16)
            for i in range(per_kv):
                at = (g * per_kv + i) * HEAD_SIZE
                dqv[h * HALF:(h + 1) * HALF, at:at + HEAD_SIZE] = dq[i * HALF:(i + 1) * HALF]

    def send_first(g, d, kinds):
        @pl.when((rank >= d) if d == reach else ((rank >= d) & jnp.logical_not(has_up)))
        def _():
            for t, r in pieces(kinds):
                sendb[g, d - 1, t, some(r), :] = owed(g, d, t, r).astype(jnp.bfloat16)
                back(g, d, t, r).start()

    def send_rest(g, kinds):
        for d in range(reach - 1, 0, -1):
            @pl.when(has_up & (rank >= d))
            def _(d=d):
                for t, r in pieces(kinds):
                    back(g, d + 1, t, r).wait_recv()
                    sendb[g, d - 1, t, some(r), :] = (
                        owed(g, d, t, r) + ret[g, d, t, some(r), :].astype(jnp.float32)
                    ).astype(jnp.bfloat16)
                    back(g, d, t, r).start()

    def finish(g, kinds):
        for t, r in pieces(kinds):
            @pl.when(has_up)
            def _(t=t, r=r):
                back(g, 1, t, r).wait_recv()
                acc[g, t, pl.ds(reach * rows + r * HALF, HALF), :] += (
                    ret[g, 0, t, some(r), :].astype(jnp.float32)
                )

            factor = scale if t == 0 else 1.0
            fin[g, t, some(r), :] = (owed(g, 0, t, r) * factor).astype(jnp.bfloat16)
            to_mate(g, t, r).start()

    for d in range(1, reach + 1):
        @pl.when(rank < d)
        def _(d=d):
            for g in range(kv_count):
                kt[g, :, slot(d)] = jnp.zeros((HEAD_SIZE, rows), jnp.bfloat16)
                stats[g, d, 0] = jnp.full((units, 2 * HALF), NEG, jnp.float32)
                stats[g, d, 1] = jnp.zeros((units, 2 * HALF), jnp.float32)
                stats[g, d, 2] = jnp.zeros((units, 2 * HALF), jnp.float32)
            for h in range(halves):
                lo, hi = part(d, h)
                dsv[h, lo:hi, :] = jnp.zeros((hi - lo, pairs * 2 * HALF), jnp.bfloat16)

    last = kv_count - 1
    seg_load.wait()
    make_bias(0)
    for copy in group_loads(0, 0):
        copy.wait()
    look_keys(0, 0)
    for d in range(1, reach):
        receive_seg(d)
    for d in range(1, reach):
        receive(0, d, 0)
    send_own(0, 1)
    for d in range(1, reach):
        biased(d)
        look_keys(0, d)
    for copy in group_loads(0, 1):
        copy.wait()
    look_values(0, 0)
    receive_seg(reach)
    biased(reach)
    for g in range(kv_count):
        more = g < last
        receive(g, reach, 0)
        look_keys(g, reach)
        combine_keys(g)
        for d in range(reach, 0, -1):
            settle(g, d, 1)
            send_first(g, d, (1,))
        for d in range(1, reach):
            receive(g, d, 1)
        if more:
            send_own(g + 1, 0)
        for d in range(1, reach):
            look_values(g, d)
        if g > 0:
            send_rest(g - 1, (0,))
            query_gradients(g - 1)
        if more:
            for copy in group_loads(g + 1, 0):
                copy.wait()
            look_keys(g + 1, 0)
        receive(g, reach, 1)
        look_values(g, reach)
        combine_values(g)
        for d in range(reach, 0, -1):
            settle(g, d, 0)
            send_first(g, d, (0,))
        if more:
            for d in range(1, reach):
                receive(g + 1, d, 0)
            send_own(g + 1, 1)
            for d in range(1, reach):
                look_keys(g + 1, d)
        send_rest(g, (1,))
        if more:
            for copy in group_loads(g + 1, 1):
                copy.wait()
            look_values(g + 1, 0)
        settle(g, 0, 1)
        settle(g, 0, 0)
    query_gradients(last)
    for g in range(last):
        finish(g, (1, 0))
    finish(last, (1,))
    send_rest(last, (0,))
    finish(last, (0,))

    for g in range(kv_count):
        for t in range(2):
            for r in range(halves):
                to_mate(g, t, r).wait()
            if shared:
                other[g, t] = (
                    fin[g, t].astype(jnp.float32) + pfin[g, t].astype(jnp.float32)
                ).astype(jnp.bfloat16)
            else:
                other[g, t] = pfin[g, t]
    for d in range(reach):
        @pl.when(has_up & (rank >= d))
        def _(d=d):
            forward_seg(d).wait_send()
            for g in range(kv_count):
                for t in range(2):
                    forward(t, g, d).wait_send()
    for d in range(1, reach + 1):
        @pl.when(rank >= d)
        def _(d=d):
            for g in range(kv_count):
                for t, r in pieces((0, 1)):
                    back(g, d, t, r).wait_send()


def place(kv_count, shared, dqv, fin, other, dq_hbm, dk_hbm, dv_hbm, sem):
    kv = lax.axis_index("kv")
    copies = [pltpu.make_async_copy(dqv, dq_hbm, sem.at[0])]
    parts = [(other, 0)] if shared else [(fin, kv * kv_count), (other, (1 - kv) * kv_count)]
    for source, base in parts:
        for g in range(kv_count):
            start = g * HEAD_SIZE
            if not shared:
                start = pl.multiple_of((base + g) * HEAD_SIZE, HEAD_SIZE)
            for t, ref in ((0, dk_hbm), (1, dv_hbm)):
                copies.append(
                    pltpu.make_async_copy(
                        source.at[g, t], ref.at[:, pl.ds(start, HEAD_SIZE)], sem.at[len(copies)]
                    )
                )
    for copy in copies:
        copy.start()
    for copy in copies:
        copy.wait()


def shards(queries, key_matrix, value_matrix, out_grad, segments):
    n = lax.axis_size("ctx")
    rows = queries.shape[0]
    head_count = queries.shape[1] // HEAD_SIZE
    group_width = QUERY_HEADS // KEY_VALUE_HEADS
    kv_count = max(head_count // group_width, 1)
    per_kv = head_count // kv_count
    kv_here = key_matrix.shape[1] // HEAD_SIZE
    shared = kv_here < kv_count * lax.axis_size("kv")
    reach = n // 2
    window = (reach + 1) * rows
    width = reach * rows + HALF
    halves = rows // HALF
    pairs = per_kv // 2
    bf16, f32 = jnp.bfloat16, jnp.float32
    dma = pltpu.SemaphoreType.DMA
    anywhere = pl.BlockSpec(memory_space=pltpu.HBM)
    inner = pltpu.VMEM
    dqv, fin, other = pl.pallas_call(
        functools.partial(kernel, n, reach, rows, per_kv, kv_count, shared),
        out_shape=(
            inner(queries.shape, bf16),
            inner((kv_count, 2, rows, HEAD_SIZE), bf16),
            inner((kv_count, 2, rows, HEAD_SIZE), bf16),
        ),
        in_specs=[anywhere] * 5,
        out_specs=(pl.BlockSpec(memory_space=pltpu.VMEM),) * 3,
        scratch_shapes=[
            pltpu.VMEM((head_count, rows, HEAD_SIZE), bf16),
            pltpu.VMEM((head_count, rows, HEAD_SIZE), bf16),
            pltpu.VMEM((kv_count, pairs, halves, width, 2 * HALF), f32),
            pltpu.VMEM((kv_count, pairs, halves, width, 2 * HALF), f32),
            pltpu.VMEM((kv_count, reach + 1, 3, pairs * halves, 2 * HALF), f32),
            pltpu.VMEM((kv_count, reach + 1, pairs * halves, 2 * HALF), f32),
            pltpu.VMEM((kv_count, pairs * halves, 2 * HALF), f32),
            pltpu.VMEM((halves, width, pairs * 2 * HALF), bf16),
            pltpu.VMEM((halves, width, pairs * 2 * HALF), bf16),
            pltpu.VMEM((2, kv_count, window, HEAD_SIZE), bf16),
            pltpu.VMEM((reach + 1, 1, rows), jnp.int32),
            pltpu.VMEM((halves, width, HALF), f32),
            pltpu.VMEM((kv_count, HEAD_SIZE, window), bf16),
            pltpu.VMEM((kv_count, 2, window, HEAD_SIZE), f32),
            pltpu.VMEM((kv_count, reach, 2, rows, HEAD_SIZE), bf16),
            pltpu.VMEM((kv_count, reach, 2, rows, HEAD_SIZE), bf16),
            pltpu.VMEM((kv_count, 2, rows, HEAD_SIZE), bf16),
            dma((1,)),
            dma((2, head_count)),
            dma((2, kv_count)),
            dma((reach + 1,)),
            dma((reach + 1,)),
            dma((2, kv_count, reach + 1)),
            dma((2, kv_count, reach + 1)),
            dma((kv_count, reach, 2, halves)),
            dma((kv_count, reach, 2, halves)),
            dma((kv_count, 2, halves)),
            dma((kv_count, 2, halves)),
        ],
        compiler_params=pltpu.CompilerParams(
            collective_id=0, has_side_effects=True, vmem_limit_bytes=56 * 1024 * 1024
        ),
    )(queries, key_matrix, value_matrix, out_grad, segments.reshape(1, rows))
    return pl.pallas_call(
        functools.partial(place, kv_count, shared),
        out_shape=(
            jax.ShapeDtypeStruct(queries.shape, bf16),
            jax.ShapeDtypeStruct(key_matrix.shape, bf16),
            jax.ShapeDtypeStruct(value_matrix.shape, bf16),
        ),
        in_specs=[pl.BlockSpec(memory_space=pltpu.VMEM)] * 3,
        out_specs=(anywhere,) * 3,
        scratch_shapes=[dma((1 + 4 * kv_count,))],
        compiler_params=pltpu.CompilerParams(vmem_limit_bytes=4 * 1024 * 1024),
    )(dqv, fin, other)


def solution(mesh):
    return jax.shard_map(
        shards,
        mesh=mesh,
        in_specs=(
            P(("groups", "ctx"), ("tp", "kv")),
            P(("groups", "ctx"), "tp"),
            P(("groups", "ctx"), "tp"),
            P(("groups", "ctx"), ("tp", "kv")),
            P(("groups", "ctx")),
        ),
        out_specs=(
            P(("groups", "ctx"), ("tp", "kv")),
            P(("groups", "ctx"), "tp"),
            P(("groups", "ctx"), "tp"),
        ),
        check_vma=False,
    )
```

```python
import functools
import jax
import jax.numpy as jnp
from jax import lax
from jax.experimental import pallas as pl
from jax.experimental.pallas import tpu as pltpu
from jax.sharding import PartitionSpec as P

QUERY_HEADS = 64
KEY_VALUE_HEADS = 8
HEAD_SIZE = 128
HALF = 128
CHUNK = 32
LOG2E = 1.4426950408889634
NEG = -1e30
MESH = pl.DeviceIdType.MESH
NT = (((1,), (1,)), ((), ()))


def kernel(
    n, reach, rows, per_kv, kv_count, shared,
    q_hbm, k_hbm, v_hbm, g_hbm, seg_hbm,
    dqv, fin, other,
    qv, gv, ev, dpv, stats, fac, deltas, pv, dsv, win, segwin, bias, kt, acc, sendb, ret, far_ret, pfin,
    seg_sem, load_sem, own_sem, seg_send, seg_recv, send_sem, recv_sem, back_send, back_recv,
    pair_send, pair_recv, far_back_send, far_back_recv,
):
    rank = lax.axis_index("ctx")
    kv = lax.axis_index("kv")
    up = lax.rem(rank + 1, n)
    down = lax.rem(rank + n - 1, n)
    mate = 1 - kv
    scale = HEAD_SIZE ** -0.5
    width = reach * rows + HALF
    halves = rows // HALF
    pairs = per_kv // 2
    first = 0 if shared else kv * kv_count

    def cols(base, g):
        if shared:
            return pl.ds(g * HEAD_SIZE, HEAD_SIZE)
        return pl.ds(pl.multiple_of((base + g) * HEAD_SIZE, HEAD_SIZE), HEAD_SIZE)

    def slot(d):
        return pl.ds((reach - d) * rows, rows)

    seg_load = pltpu.make_async_copy(seg_hbm, segwin.at[0], seg_sem.at[0])

    def own(t, g):
        ref = k_hbm if t == 0 else v_hbm
        return pltpu.make_async_copy(
            ref.at[:, cols(first, g)], win.at[t, g, slot(0)], own_sem.at[t, g]
        )

    def load(t, head):
        ref, to = ((q_hbm, qv), (g_hbm, gv))[t]
        return pltpu.make_async_copy(
            ref.at[:, pl.ds(head * HEAD_SIZE, HEAD_SIZE)], to.at[head], load_sem.at[t, head]
        )

    def group_loads(g, t):
        return [own(t, g)] + [load(t, i) for i in range(g * per_kv, (g + 1) * per_kv)]

    def forward(t, g, d):
        ref = k_hbm if t == 0 else v_hbm
        src = ref.at[:, cols(first, g)] if d == 0 else win.at[t, g, slot(d)]
        return pltpu.make_async_remote_copy(
            src_ref=src,
            dst_ref=win.at[t, g, slot(d + 1)],
            send_sem=send_sem.at[t, g, d],
            recv_sem=recv_sem.at[t, g, d + 1],
            device_id={"ctx": up},
            device_id_type=MESH,
        )

    def forward_seg(d):
        return pltpu.make_async_remote_copy(
            src_ref=seg_hbm if d == 0 else segwin.at[d],
            dst_ref=segwin.at[d + 1],
            send_sem=seg_send.at[d],
            recv_sem=seg_recv.at[d + 1],
            device_id={"ctx": up},
            device_id_type=MESH,
        )

    def pieces(kinds):
        return [(t, r) for t in kinds for r in range(halves)]

    def some(r):
        return pl.ds(r * HALF, HALF)

    def back(g, d, t, r):
        return pltpu.make_async_remote_copy(
            src_ref=sendb.at[g, d - 1, t, some(r)],
            dst_ref=ret.at[g, d - 1, t, some(r)],
            send_sem=back_send.at[g, d - 1, t, r],
            recv_sem=back_recv.at[g, d - 1, t, r],
            device_id={"ctx": down},
            device_id_type=MESH,
        )

    def back_far(g, t, r):
        return pltpu.make_async_remote_copy(
            src_ref=sendb.at[g, 1, t, some(r)],
            dst_ref=far_ret.at[g, t, some(r)],
            send_sem=far_back_send.at[g, t, r],
            recv_sem=far_back_recv.at[g, t, r],
            device_id={"ctx": lax.rem(rank + n - 2, n)},
            device_id_type=MESH,
        )

    far = reach > 1

    def goes_far(of, g, t):
        yes = of == 2
        if g == kv_count - 1 and t in ():
            yes = yes | (of == n - 1)
        return yes

    def owed(g, d, t, r):
        return acc[g, t, pl.ds((reach - d) * rows + r * HALF, HALF), :]

    def to_mate(g, t, r):
        return pltpu.make_async_remote_copy(
            src_ref=fin.at[g, t, some(r)],
            dst_ref=pfin.at[g, t, some(r)],
            send_sem=pair_send.at[g, t, r],
            recv_sem=pair_recv.at[g, t, r],
            device_id={"kv": mate},
            device_id_type=MESH,
        )

    has_up = rank < n - 1

    seg_load.start()
    for g in range(kv_count):
        for t in range(2):
            for copy in group_loads(g, t):
                copy.start()

    barrier = pltpu.get_barrier_semaphore()
    pl.semaphore_signal(barrier, inc=1, device_id={"kv": mate}, device_id_type=MESH)

    @pl.when(has_up)
    def _():
        pl.semaphore_signal(barrier, inc=1, device_id={"ctx": up}, device_id_type=MESH)

    @pl.when(rank > 0)
    def _():
        pl.semaphore_signal(barrier, inc=1, device_id={"ctx": down}, device_id_type=MESH)

    expected = 1 + jnp.where(has_up, 1, 0) + jnp.where(rank > 0, 1, 0)
    if far:
        @pl.when(rank == 0)
        def _():
            pl.semaphore_signal(
                barrier, inc=1, device_id={"ctx": lax.rem(rank + 2, n)}, device_id_type=MESH
            )

        expected = expected + jnp.where(rank == 2, 1, 0)
    pl.semaphore_wait(barrier, expected)

    @pl.when(has_up)
    def _():
        forward_seg(0).start()
        forward(0, 0, 0).start()
        forward(1, 0, 0).start()

    units = pairs * halves

    def receive_seg(d):
        @pl.when(rank >= d)
        def _():
            forward_seg(d - 1).wait_recv()

        if d < reach:
            @pl.when((rank >= d) & has_up)
            def _():
                forward_seg(d).start()

    def receive(g, d, t):
        @pl.when(rank >= d)
        def _():
            forward(t, g, d - 1).wait_recv()

        if d < reach:
            @pl.when((rank >= d) & has_up)
            def _():
                forward(t, g, d).start()

    def send_own(g, t):
        @pl.when(has_up)
        def _():
            forward(t, g, 0).start()

    def part(d, h):
        start = (reach - d) * rows - h * HALF
        return max(start, 0), min(start + rows, width)

    def make_bias(d):
        column = jnp.broadcast_to(segwin[d].astype(jnp.float32), (HALF, rows)).T
        for h in range(halves):
            lo, hi = part(d, h)
            begin = lo + h * HALF - (reach - d) * rows
            seg_q = segwin[0, :, h * HALF:(h + 1) * HALF].astype(jnp.float32)
            keep = column[begin:begin + hi - lo] == seg_q
            if d == 0:
                key_at = lax.broadcasted_iota(jnp.int32, (hi - lo, HALF), 0)
                query_at = lax.broadcasted_iota(jnp.int32, (hi - lo, HALF), 1)
                keep = keep & (key_at + begin <= query_at + h * HALF)
            bias[h, lo:hi, :] = jnp.where(keep, 0.0, NEG)

    def biased(d):
        @pl.when(rank >= d)
        def _():
            make_bias(d)

    def pair(ref, g, h, p):
        head = g * per_kv + 2 * p
        return ref[head:head + 2, h * HALF:(h + 1) * HALF, :].reshape(2 * HALF, HEAD_SIZE)

    def stack(ref, g, h):
        return ref[g * per_kv:(g + 1) * per_kv, h * HALF:(h + 1) * HALF, :].reshape(
            per_kv * HALF, HEAD_SIZE
        )

    def key_products(g, d, p, h):
        lo, hi = part(d, h)
        span = slice(lo + h * HALF, hi + h * HALF)
        s = lax.dot_general(
            win[0, g, span, :], pair(qv, g, h, p), NT, preferred_element_type=jnp.float32
        )
        b = bias[h, lo:hi, :]
        s = s + jnp.concatenate([b, b], axis=1)
        ev[g, p, h, lo:hi, :] = s
        u = p * halves + h
        stats[g, d, 0, u:u + 1, :] = jnp.max(s, axis=0, keepdims=True)

    def exponentials(g, d, p, h):
        lo, hi = part(d, h)
        u = p * halves + h
        peak = stats[g, d, 0, u:u + 1, :]
        total = jnp.zeros((8, 2 * HALF), jnp.float32)
        for c in range(lo, hi, CHUNK):
            at = slice(c, c + CHUNK)
            e = jnp.exp2((ev[g, p, h, at, :] - peak) * (scale * LOG2E))
            ev[g, p, h, at, :] = e
            total = total + jnp.sum(e.reshape(-1, 8, 2 * HALF), axis=0)
        stats[g, d, 1, u:u + 1, :] = jnp.sum(total, axis=0, keepdims=True)

    def value_products(g, d, p, h):
        lo, hi = part(d, h)
        span = slice(lo + h * HALF, hi + h * HALF)
        u = p * halves + h
        dp = lax.dot_general(
            win[1, g, span, :], pair(gv, g, h, p), NT, preferred_element_type=jnp.float32
        )
        dpv[g, p, h, lo:hi, :] = dp
        stats[g, d, 2, u:u + 1, :] = jnp.sum(ev[g, p, h, lo:hi, :] * dp, axis=0, keepdims=True)

    todo = [(p, h) for p in range(pairs) for h in range(halves)]

    def look_keys(g, d):
        @pl.when(rank >= d)
        def _():
            key_products(g, d, *todo[0])
            for i, at in enumerate(todo):
                if i + 1 < len(todo):
                    key_products(g, d, *todo[i + 1])
                exponentials(g, d, *at)

    def look_values(g, d):
        @pl.when(rank >= d)
        def _():
            for at in todo:
                value_products(g, d, *at)

    def combine_keys(g):
        peak = stats[g, 0, 0]
        for d in range(1, reach + 1):
            peak = jnp.maximum(peak, stats[g, d, 0])
        total = jnp.zeros((units, 2 * HALF), jnp.float32)
        for d in range(reach + 1):
            f = jnp.exp2((stats[g, d, 0] - peak) * (scale * LOG2E))
            fac[g, d] = f
            total = total + f * stats[g, d, 1]
        inv = 1.0 / total
        for d in range(reach + 1):
            fac[g, d] = fac[g, d] * inv

    def combine_values(g):
        weighted = jnp.zeros((units, 2 * HALF), jnp.float32)
        for d in range(reach + 1):
            weighted = weighted + fac[g, d] * stats[g, d, 2]
        deltas[g] = weighted

    def settle(g, d, t):
        @pl.when(rank >= d)
        def _():
            order = list(range(halves)) if d > 0 else list(range(halves - 1, -1, -1))
            for i, h in enumerate(order):
                lo, hi = part(d, h)
                for p in range(pairs):
                    u = p * halves + h
                    f = fac[g, d, u:u + 1, :]
                    there = slice(p * 2 * HALF, (p + 1) * 2 * HALF)
                    for c in range(lo, hi, CHUNK):
                        at = slice(c, c + CHUNK)
                        pn = ev[g, p, h, at, :] * f
                        if t == 0:
                            delta = deltas[g, u:u + 1, :]
                            dsv[g, h, at, there] = (
                                pn * (dpv[g, p, h, at, :] - delta)
                            ).astype(jnp.bfloat16)
                        else:
                            pv[h, at, there] = pn.astype(jnp.bfloat16)
            for i, h in enumerate(order):
                lo, hi = part(d, h)
                span = slice(lo + h * HALF, hi + h * HALF)
                low, ref = ((dsv.at[g], qv), (pv, gv))[t]
                out = jnp.dot(
                    low[h, lo:hi, :], stack(ref, g, h), preferred_element_type=jnp.float32
                )
                if i > 0:
                    acc[g, t, span, :] += out
                else:
                    acc[g, t, span, :] = out

    def query_gradients(g):
        for d in range(reach + 1):
            @pl.when(rank >= d)
            def _(d=d):
                kt[g, :, slot(d)] = win[0, g, slot(d), :].T
        for h in range(halves):
            dqt = jnp.dot(
                kt[g, :, h * HALF:h * HALF + width], dsv[g, h], preferred_element_type=jnp.float32
            )
            dq = (dqt * scale).T.astype(jnp.bfloat16)
            for i in range(per_kv):
                at = (g * per_kv + i) * HEAD_SIZE
                dqv[h * HALF:(h + 1) * HALF, at:at + HEAD_SIZE] = dq[i * HALF:(i + 1) * HALF]

    def start_back(g, d, t, r):
        if far and d == 2:
            away = goes_far(rank, g, t)

            @pl.when(away)
            def _():
                back_far(g, t, r).start()

            @pl.when(jnp.logical_not(away))
            def _():
                back(g, d, t, r).start()
        else:
            back(g, d, t, r).start()

    def alone(g, d, t):
        if d == reach:
            return rank >= d
        yes = jnp.logical_not(has_up)
        if far and d == 1:
            yes = yes | goes_far(rank + 1, g, t)
        return (rank >= d) & yes

    def send_first(g, d, kinds):
        for t in kinds:
            @pl.when(alone(g, d, t))
            def _(t=t):
                for r in range(halves):
                    sendb[g, d - 1, t, some(r), :] = owed(g, d, t, r).astype(jnp.bfloat16)
                for r in range(halves):
                    start_back(g, d, t, r)

    def send_rest(g, kinds):
        for d in range(reach - 1, 0, -1):
            for t in kinds:
                @pl.when((rank >= d) & jnp.logical_not(alone(g, d, t)))
                def _(d=d, t=t):
                    for r in range(halves):
                        back(g, d + 1, t, r).wait_recv()
                        sendb[g, d - 1, t, some(r), :] = (
                            owed(g, d, t, r) + ret[g, d, t, some(r), :].astype(jnp.float32)
                        ).astype(jnp.bfloat16)
                        start_back(g, d, t, r)

    def finish(g, kinds):
        for t, r in pieces(kinds):
            @pl.when(has_up)
            def _(t=t, r=r):
                back(g, 1, t, r).wait_recv()
                acc[g, t, pl.ds(reach * rows + r * HALF, HALF), :] += (
                    ret[g, 0, t, some(r), :].astype(jnp.float32)
                )

            if far:
                @pl.when(goes_far(rank + 2, g, t))
                def _(t=t, r=r):
                    back_far(g, t, r).wait_recv()
                    acc[g, t, pl.ds(reach * rows + r * HALF, HALF), :] += (
                        far_ret[g, t, some(r), :].astype(jnp.float32)
                    )

            factor = scale if t == 0 else 1.0
            fin[g, t, some(r), :] = (owed(g, 0, t, r) * factor).astype(jnp.bfloat16)
            to_mate(g, t, r).start()

    for d in range(1, reach + 1):
        @pl.when(rank < d)
        def _(d=d):
            for g in range(kv_count):
                kt[g, :, slot(d)] = jnp.zeros((HEAD_SIZE, rows), jnp.bfloat16)
                stats[g, d, 0] = jnp.full((units, 2 * HALF), NEG, jnp.float32)
                stats[g, d, 1] = jnp.zeros((units, 2 * HALF), jnp.float32)
                stats[g, d, 2] = jnp.zeros((units, 2 * HALF), jnp.float32)
            for h in range(halves):
                lo, hi = part(d, h)
                for g in range(kv_count):
                    dsv[g, h, lo:hi, :] = jnp.zeros(
                        (hi - lo, pairs * 2 * HALF), jnp.bfloat16
                    )

    last = kv_count - 1
    def ready(g, t):
        for copy in group_loads(g, t):
            copy.wait()

    seg_load.wait()
    make_bias(0)
    ready(0, 0)
    look_keys(0, 0)
    for d in range(1, reach):
        receive_seg(d)
    for d in range(1, reach):
        receive(0, d, 0)
        biased(d)
        look_keys(0, d)
    ready(0, 1)
    look_values(0, 0)
    for d in range(1, reach):
        receive(0, d, 1)
    if last > 0:
        for t in range(2):
            send_own(1, t)
    for d in range(1, reach):
        look_values(0, d)
    receive_seg(reach)
    biased(reach)
    for g in range(kv_count):
        more = g < last
        if more:
            ready(g + 1, 0)
            look_keys(g + 1, 0)
        receive(g, reach, 0)
        look_keys(g, reach)
        combine_keys(g)
        settle(g, reach, 1)
        send_first(g, reach, (1,))
        for d in range(reach - 1, 0, -1):
            settle(g, d, 1)
            if more:
                send_first(g, d, (1,))
        if g > 0:
            send_rest(g - 1, (1,))
        receive(g, reach, 1)
        look_values(g, reach)
        combine_values(g)
        settle(g, reach, 0)
        send_first(g, reach, (0,))
        for d in range(reach - 1, 0, -1):
            if not more:
                send_first(g, d, (1,))
            settle(g, d, 0)
            send_first(g, d, (0,))
        if more:
            for d in range(1, reach):
                receive(g + 1, d, 0)
                look_keys(g + 1, d)
            ready(g + 1, 1)
            look_values(g + 1, 0)
            for d in range(1, reach):
                receive(g + 1, d, 1)
            if g + 2 < kv_count:
                for t in range(2):
                    send_own(g + 2, t)
            for d in range(1, reach):
                look_values(g + 1, d)
        if g > 0:
            send_rest(g - 1, (0,))
        settle(g, 0, 1)
        settle(g, 0, 0)
    for g in range(kv_count):
        query_gradients(g)
    send_rest(last, (1,))
    for g in range(last):
        finish(g, (1, 0))
    finish(last, (1,))
    send_rest(last, (0,))
    finish(last, (0,))

    for g in range(kv_count):
        for t in range(2):
            for r in range(halves):
                to_mate(g, t, r).wait()
            if shared:
                other[g, t] = (
                    fin[g, t].astype(jnp.float32) + pfin[g, t].astype(jnp.float32)
                ).astype(jnp.bfloat16)
            else:
                other[g, t] = pfin[g, t]
    for d in range(reach):
        @pl.when(has_up & (rank >= d))
        def _(d=d):
            forward_seg(d).wait_send()
            for g in range(kv_count):
                for t in range(2):
                    forward(t, g, d).wait_send()
    for d in range(1, reach + 1):
        for g in range(kv_count):
            for t in range(2):
                if far and d == 2:
                    @pl.when(goes_far(rank, g, t))
                    def _(g=g, t=t):
                        for r in range(halves):
                            back_far(g, t, r).wait_send()

                    @pl.when((rank >= d) & jnp.logical_not(goes_far(rank, g, t)))
                    def _(g=g, t=t, d=d):
                        for r in range(halves):
                            back(g, d, t, r).wait_send()
                else:
                    @pl.when(rank >= d)
                    def _(g=g, t=t, d=d):
                        for r in range(halves):
                            back(g, d, t, r).wait_send()


def place(kv_count, shared, dqv, fin, other, dq_hbm, dk_hbm, dv_hbm, sem):
    kv = lax.axis_index("kv")
    copies = [pltpu.make_async_copy(dqv, dq_hbm, sem.at[0])]
    parts = [(other, 0)] if shared else [(fin, kv * kv_count), (other, (1 - kv) * kv_count)]
    for source, base in parts:
        for g in range(kv_count):
            start = g * HEAD_SIZE
            if not shared:
                start = pl.multiple_of((base + g) * HEAD_SIZE, HEAD_SIZE)
            for t, ref in ((0, dk_hbm), (1, dv_hbm)):
                copies.append(
                    pltpu.make_async_copy(
                        source.at[g, t], ref.at[:, pl.ds(start, HEAD_SIZE)], sem.at[len(copies)]
                    )
                )
    for copy in copies:
        copy.start()
    for copy in copies:
        copy.wait()


def shards(queries, key_matrix, value_matrix, out_grad, segments):
    n = lax.axis_size("ctx")
    rows = queries.shape[0]
    head_count = queries.shape[1] // HEAD_SIZE
    group_width = QUERY_HEADS // KEY_VALUE_HEADS
    kv_count = max(head_count // group_width, 1)
    per_kv = head_count // kv_count
    kv_here = key_matrix.shape[1] // HEAD_SIZE
    shared = kv_here < kv_count * lax.axis_size("kv")
    reach = n // 2
    window = (reach + 1) * rows
    width = reach * rows + HALF
    halves = rows // HALF
    pairs = per_kv // 2
    bf16, f32 = jnp.bfloat16, jnp.float32
    dma = pltpu.SemaphoreType.DMA
    anywhere = pl.BlockSpec(memory_space=pltpu.HBM)
    inner = pltpu.VMEM
    dqv, fin, other = pl.pallas_call(
        functools.partial(kernel, n, reach, rows, per_kv, kv_count, shared),
        out_shape=(
            inner(queries.shape, bf16),
            inner((kv_count, 2, rows, HEAD_SIZE), bf16),
            inner((kv_count, 2, rows, HEAD_SIZE), bf16),
        ),
        in_specs=[anywhere] * 5,
        out_specs=(pl.BlockSpec(memory_space=pltpu.VMEM),) * 3,
        scratch_shapes=[
            pltpu.VMEM((head_count, rows, HEAD_SIZE), bf16),
            pltpu.VMEM((head_count, rows, HEAD_SIZE), bf16),
            pltpu.VMEM((kv_count, pairs, halves, width, 2 * HALF), f32),
            pltpu.VMEM((kv_count, pairs, halves, width, 2 * HALF), f32),
            pltpu.VMEM((kv_count, reach + 1, 3, pairs * halves, 2 * HALF), f32),
            pltpu.VMEM((kv_count, reach + 1, pairs * halves, 2 * HALF), f32),
            pltpu.VMEM((kv_count, pairs * halves, 2 * HALF), f32),
            pltpu.VMEM((halves, width, pairs * 2 * HALF), bf16),
            pltpu.VMEM((kv_count, halves, width, pairs * 2 * HALF), bf16),
            pltpu.VMEM((2, kv_count, window, HEAD_SIZE), bf16),
            pltpu.VMEM((reach + 1, 1, rows), jnp.int32),
            pltpu.VMEM((halves, width, HALF), f32),
            pltpu.VMEM((kv_count, HEAD_SIZE, window), bf16),
            pltpu.VMEM((kv_count, 2, window, HEAD_SIZE), f32),
            pltpu.VMEM((kv_count, reach, 2, rows, HEAD_SIZE), bf16),
            pltpu.VMEM((kv_count, reach, 2, rows, HEAD_SIZE), bf16),
            pltpu.VMEM((kv_count, 2, rows, HEAD_SIZE), bf16),
            pltpu.VMEM((kv_count, 2, rows, HEAD_SIZE), bf16),
            dma((1,)),
            dma((2, head_count)),
            dma((2, kv_count)),
            dma((reach + 1,)),
            dma((reach + 1,)),
            dma((2, kv_count, reach + 1)),
            dma((2, kv_count, reach + 1)),
            dma((kv_count, reach, 2, halves)),
            dma((kv_count, reach, 2, halves)),
            dma((kv_count, 2, halves)),
            dma((kv_count, 2, halves)),
            dma((kv_count, 2, halves)),
            dma((kv_count, 2, halves)),
        ],
        compiler_params=pltpu.CompilerParams(
            collective_id=0, has_side_effects=True, vmem_limit_bytes=56 * 1024 * 1024
        ),
    )(queries, key_matrix, value_matrix, out_grad, segments.reshape(1, rows))
    return pl.pallas_call(
        functools.partial(place, kv_count, shared),
        out_shape=(
            jax.ShapeDtypeStruct(queries.shape, bf16),
            jax.ShapeDtypeStruct(key_matrix.shape, bf16),
            jax.ShapeDtypeStruct(value_matrix.shape, bf16),
        ),
        in_specs=[pl.BlockSpec(memory_space=pltpu.VMEM)] * 3,
        out_specs=(anywhere,) * 3,
        scratch_shapes=[dma((1 + 4 * kv_count,))],
        compiler_params=pltpu.CompilerParams(vmem_limit_bytes=4 * 1024 * 1024),
    )(dqv, fin, other)


def solution(mesh):
    return jax.shard_map(
        shards,
        mesh=mesh,
        in_specs=(
            P(("groups", "ctx"), ("tp", "kv")),
            P(("groups", "ctx"), "tp"),
            P(("groups", "ctx"), "tp"),
            P(("groups", "ctx"), ("tp", "kv")),
            P(("groups", "ctx")),
        ),
        out_specs=(
            P(("groups", "ctx"), ("tp", "kv")),
            P(("groups", "ctx"), "tp"),
            P(("groups", "ctx"), "tp"),
        ),
        check_vma=False,
    )
```

```python
import functools
import jax
import jax.numpy as jnp
from jax import lax
from jax.experimental import pallas as pl
from jax.experimental.pallas import tpu as pltpu
from jax.sharding import PartitionSpec as P

QUERY_HEADS = 64
KEY_VALUE_HEADS = 8
HEAD_SIZE = 128
HALF = 128
CHUNK = 32
LOG2E = 1.4426950408889634
NEG = -1e30
MESH = pl.DeviceIdType.MESH
NT = (((1,), (1,)), ((), ()))


def kernel(
    n, reach, rows, per_kv, kv_count, shared,
    q_hbm, k_hbm, v_hbm, g_hbm, seg_hbm,
    dqv, fin, other,
    qv, gv, ev, dpv, stats, fac, deltas, pv, dsv, win, segwin, bias, kt, acc, sendb, ret, far_ret, pfin,
    seg_sem, load_sem, own_sem, seg_send, seg_recv, send_sem, recv_sem, back_send, back_recv,
    pair_send, pair_recv, far_back_send, far_back_recv,
):
    rank = lax.axis_index("ctx")
    kv = lax.axis_index("kv")
    up = lax.rem(rank + 1, n)
    down = lax.rem(rank + n - 1, n)
    mate = 1 - kv
    scale = HEAD_SIZE ** -0.5
    width = reach * rows + HALF
    halves = rows // HALF
    pairs = per_kv // 2
    first = 0 if shared else kv * kv_count

    def cols(base, g):
        if shared:
            return pl.ds(g * HEAD_SIZE, HEAD_SIZE)
        return pl.ds(pl.multiple_of((base + g) * HEAD_SIZE, HEAD_SIZE), HEAD_SIZE)

    def slot(d):
        return pl.ds((reach - d) * rows, rows)

    seg_load = pltpu.make_async_copy(seg_hbm, segwin.at[0], seg_sem.at[0])

    def own(t, g):
        ref = k_hbm if t == 0 else v_hbm
        return pltpu.make_async_copy(
            ref.at[:, cols(first, g)], win.at[t, g, slot(0)], own_sem.at[t, g]
        )

    def load(t, head):
        ref, to = ((q_hbm, qv), (g_hbm, gv))[t]
        return pltpu.make_async_copy(
            ref.at[:, pl.ds(head * HEAD_SIZE, HEAD_SIZE)], to.at[head], load_sem.at[t, head]
        )

    def group_loads(g, t):
        return [own(t, g)] + [load(t, i) for i in range(g * per_kv, (g + 1) * per_kv)]

    def some(r):
        return pl.ds(r * HALF, HALF)

    def forward(t, g, d, r):
        ref = k_hbm if t == 0 else v_hbm
        at = (reach - d) * rows + r * HALF
        src = ref.at[some(r), cols(first, g)] if d == 0 else win.at[t, g, pl.ds(at, HALF)]
        return pltpu.make_async_remote_copy(
            src_ref=src,
            dst_ref=win.at[t, g, pl.ds(at - rows, HALF)],
            send_sem=send_sem.at[t, g, d, r],
            recv_sem=recv_sem.at[t, g, d + 1, r],
            device_id={"ctx": up},
            device_id_type=MESH,
        )

    def forward_seg(d):
        return pltpu.make_async_remote_copy(
            src_ref=seg_hbm if d == 0 else segwin.at[d],
            dst_ref=segwin.at[d + 1],
            send_sem=seg_send.at[d],
            recv_sem=seg_recv.at[d + 1],
            device_id={"ctx": up},
            device_id_type=MESH,
        )

    def pieces(kinds):
        return [(t, r) for t in kinds for r in range(halves)]

    def back(g, d, t, r):
        return pltpu.make_async_remote_copy(
            src_ref=sendb.at[g, d - 1, t, some(r)],
            dst_ref=ret.at[g, d - 1, t, some(r)],
            send_sem=back_send.at[g, d - 1, t, r],
            recv_sem=back_recv.at[g, d - 1, t, r],
            device_id={"ctx": down},
            device_id_type=MESH,
        )

    def back_far(g, t, r):
        return pltpu.make_async_remote_copy(
            src_ref=sendb.at[g, 1, t, some(r)],
            dst_ref=far_ret.at[g, t, some(r)],
            send_sem=far_back_send.at[g, t, r],
            recv_sem=far_back_recv.at[g, t, r],
            device_id={"ctx": lax.rem(rank + n - 2, n)},
            device_id_type=MESH,
        )

    far = reach > 1

    def goes_far(of, g, t):
        yes = of == 2
        if g == kv_count - 1 and t in ():
            yes = yes | (of == n - 1)
        return yes

    def owed(g, d, t, r):
        return acc[g, t, pl.ds((reach - d) * rows + r * HALF, HALF), :]

    def to_mate(g, t, r):
        return pltpu.make_async_remote_copy(
            src_ref=fin.at[g, t, some(r)],
            dst_ref=pfin.at[g, t, some(r)],
            send_sem=pair_send.at[g, t, r],
            recv_sem=pair_recv.at[g, t, r],
            device_id={"kv": mate},
            device_id_type=MESH,
        )

    has_up = rank < n - 1

    barrier = pltpu.get_barrier_semaphore()
    pl.semaphore_signal(barrier, inc=1, device_id={"kv": mate}, device_id_type=MESH)

    @pl.when(has_up)
    def _():
        pl.semaphore_signal(barrier, inc=1, device_id={"ctx": up}, device_id_type=MESH)

    @pl.when(rank > 0)
    def _():
        pl.semaphore_signal(barrier, inc=1, device_id={"ctx": down}, device_id_type=MESH)

    expected = 1 + jnp.where(has_up, 1, 0) + jnp.where(rank > 0, 1, 0)
    if far:
        @pl.when(rank == 0)
        def _():
            pl.semaphore_signal(
                barrier, inc=1, device_id={"ctx": lax.rem(rank + 2, n)}, device_id_type=MESH
            )

        expected = expected + jnp.where(rank == 2, 1, 0)
    seg_load.start()
    for g in range(kv_count):
        for t in range(2):
            for copy in group_loads(g, t):
                copy.start()

    pl.semaphore_wait(barrier, expected)

    @pl.when(has_up)
    def _():
        forward_seg(0).start()
        for t in range(2):
            for r in range(halves):
                forward(t, 0, 0, r).start()

    units = pairs * halves

    def receive_seg(d):
        @pl.when(rank >= d)
        def _():
            forward_seg(d - 1).wait_recv()

        if d < reach:
            @pl.when((rank >= d) & has_up)
            def _():
                forward_seg(d).start()

    def receive(g, d, t):
        for r in range(halves):
            @pl.when(rank >= d)
            def _(r=r):
                forward(t, g, d - 1, r).wait_recv()

            if d < reach:
                @pl.when((rank >= d) & has_up)
                def _(r=r):
                    forward(t, g, d, r).start()

    def send_own(g, t):
        @pl.when(has_up)
        def _():
            for r in range(halves):
                forward(t, g, 0, r).start()

    def part(d, h):
        start = (reach - d) * rows - h * HALF
        return max(start, 0), min(start + rows, width)

    def make_bias(d):
        column = jnp.broadcast_to(segwin[d].astype(jnp.float32), (HALF, rows)).T
        for h in range(halves):
            lo, hi = part(d, h)
            begin = lo + h * HALF - (reach - d) * rows
            seg_q = segwin[0, :, h * HALF:(h + 1) * HALF].astype(jnp.float32)
            keep = column[begin:begin + hi - lo] == seg_q
            if d == 0:
                key_at = lax.broadcasted_iota(jnp.int32, (hi - lo, HALF), 0)
                query_at = lax.broadcasted_iota(jnp.int32, (hi - lo, HALF), 1)
                keep = keep & (key_at + begin <= query_at + h * HALF)
            bias[h, lo:hi, :] = jnp.where(keep, 0.0, NEG)

    def biased(d):
        @pl.when(rank >= d)
        def _():
            make_bias(d)

    def pair(ref, g, h, p):
        head = g * per_kv + 2 * p
        return ref[head:head + 2, h * HALF:(h + 1) * HALF, :].reshape(2 * HALF, HEAD_SIZE)

    def stack(ref, g, h):
        return ref[g * per_kv:(g + 1) * per_kv, h * HALF:(h + 1) * HALF, :].reshape(
            per_kv * HALF, HEAD_SIZE
        )

    def key_products(g, d, p, h):
        lo, hi = part(d, h)
        span = slice(lo + h * HALF, hi + h * HALF)
        s = lax.dot_general(
            win[0, g, span, :], pair(qv, g, h, p), NT, preferred_element_type=jnp.float32
        )
        b = bias[h, lo:hi, :]
        s = s + jnp.concatenate([b, b], axis=1)
        ev[g, p, h, lo:hi, :] = s
        u = p * halves + h
        stats[g, d, 0, u:u + 1, :] = jnp.max(s, axis=0, keepdims=True)

    def exponentials(g, d, p, h):
        lo, hi = part(d, h)
        u = p * halves + h
        peak = stats[g, d, 0, u:u + 1, :]
        total = jnp.zeros((8, 2 * HALF), jnp.float32)
        for c in range(lo, hi, CHUNK):
            at = slice(c, c + CHUNK)
            e = jnp.exp2((ev[g, p, h, at, :] - peak) * (scale * LOG2E))
            ev[g, p, h, at, :] = e
            total = total + jnp.sum(e.reshape(-1, 8, 2 * HALF), axis=0)
        stats[g, d, 1, u:u + 1, :] = jnp.sum(total, axis=0, keepdims=True)

    def value_products(g, d, p, h):
        lo, hi = part(d, h)
        span = slice(lo + h * HALF, hi + h * HALF)
        u = p * halves + h
        dp = lax.dot_general(
            win[1, g, span, :], pair(gv, g, h, p), NT, preferred_element_type=jnp.float32
        )
        dpv[g, p, h, lo:hi, :] = dp
        stats[g, d, 2, u:u + 1, :] = jnp.sum(ev[g, p, h, lo:hi, :] * dp, axis=0, keepdims=True)

    todo = [(p, h) for p in range(pairs) for h in range(halves)]

    def look_keys(g, d):
        @pl.when(rank >= d)
        def _():
            key_products(g, d, *todo[0])
            for i, at in enumerate(todo):
                if i + 1 < len(todo):
                    key_products(g, d, *todo[i + 1])
                exponentials(g, d, *at)

    def look_values(g, d):
        @pl.when(rank >= d)
        def _():
            for at in todo:
                value_products(g, d, *at)

    def combine_keys(g):
        peak = stats[g, 0, 0]
        for d in range(1, reach + 1):
            peak = jnp.maximum(peak, stats[g, d, 0])
        total = jnp.zeros((units, 2 * HALF), jnp.float32)
        for d in range(reach + 1):
            f = jnp.exp2((stats[g, d, 0] - peak) * (scale * LOG2E))
            fac[g, d] = f
            total = total + f * stats[g, d, 1]
        inv = 1.0 / total
        for d in range(reach + 1):
            fac[g, d] = fac[g, d] * inv

    def combine_values(g):
        weighted = jnp.zeros((units, 2 * HALF), jnp.float32)
        for d in range(reach + 1):
            weighted = weighted + fac[g, d] * stats[g, d, 2]
        deltas[g] = weighted

    def settle(g, d, t):
        @pl.when(rank >= d)
        def _():
            order = list(range(halves)) if d > 0 else list(range(halves - 1, -1, -1))
            for i, h in enumerate(order):
                lo, hi = part(d, h)
                for p in range(pairs):
                    u = p * halves + h
                    f = fac[g, d, u:u + 1, :]
                    there = slice(p * 2 * HALF, (p + 1) * 2 * HALF)
                    for c in range(lo, hi, CHUNK):
                        at = slice(c, c + CHUNK)
                        pn = ev[g, p, h, at, :] * f
                        if t == 0:
                            delta = deltas[g, u:u + 1, :]
                            dsv[g, h, at, there] = (
                                pn * (dpv[g, p, h, at, :] - delta)
                            ).astype(jnp.bfloat16)
                        else:
                            pv[h, at, there] = pn.astype(jnp.bfloat16)
            for i, h in enumerate(order):
                lo, hi = part(d, h)
                span = slice(lo + h * HALF, hi + h * HALF)
                low, ref = ((dsv.at[g], qv), (pv, gv))[t]
                out = jnp.dot(
                    low[h, lo:hi, :], stack(ref, g, h), preferred_element_type=jnp.float32
                )
                if i > 0:
                    acc[g, t, span, :] += out
                else:
                    acc[g, t, span, :] = out

    def query_gradients(g):
        for d in range(reach + 1):
            @pl.when(rank >= d)
            def _(d=d):
                kt[g, :, slot(d)] = win[0, g, slot(d), :].T
        for h in range(halves):
            dqt = jnp.dot(
                kt[g, :, h * HALF:h * HALF + width], dsv[g, h], preferred_element_type=jnp.float32
            )
            dq = (dqt * scale).T.astype(jnp.bfloat16)
            for i in range(per_kv):
                at = (g * per_kv + i) * HEAD_SIZE
                dqv[h * HALF:(h + 1) * HALF, at:at + HEAD_SIZE] = dq[i * HALF:(i + 1) * HALF]

    def start_back(g, d, t, r):
        if far and d == 2:
            away = goes_far(rank, g, t)

            @pl.when(away)
            def _():
                back_far(g, t, r).start()

            @pl.when(jnp.logical_not(away))
            def _():
                back(g, d, t, r).start()
        else:
            back(g, d, t, r).start()

    def alone(g, d, t):
        if d == reach:
            return rank >= d
        yes = jnp.logical_not(has_up)
        if far and d == 1:
            yes = yes | goes_far(rank + 1, g, t)
        return (rank >= d) & yes

    def send_first(g, d, kinds):
        for t in kinds:
            @pl.when(alone(g, d, t))
            def _(t=t):
                for r in range(halves):
                    sendb[g, d - 1, t, some(r), :] = owed(g, d, t, r).astype(jnp.bfloat16)
                for r in range(halves):
                    start_back(g, d, t, r)

    def send_rest(g, kinds):
        for d in range(reach - 1, 0, -1):
            for t in kinds:
                @pl.when((rank >= d) & jnp.logical_not(alone(g, d, t)))
                def _(d=d, t=t):
                    for r in range(halves):
                        back(g, d + 1, t, r).wait_recv()
                        sendb[g, d - 1, t, some(r), :] = (
                            owed(g, d, t, r) + ret[g, d, t, some(r), :].astype(jnp.float32)
                        ).astype(jnp.bfloat16)
                        start_back(g, d, t, r)

    def finish(g, kinds):
        for t, r in pieces(kinds):
            @pl.when(has_up)
            def _(t=t, r=r):
                back(g, 1, t, r).wait_recv()
                acc[g, t, pl.ds(reach * rows + r * HALF, HALF), :] += (
                    ret[g, 0, t, some(r), :].astype(jnp.float32)
                )

            if far:
                @pl.when(goes_far(rank + 2, g, t))
                def _(t=t, r=r):
                    back_far(g, t, r).wait_recv()
                    acc[g, t, pl.ds(reach * rows + r * HALF, HALF), :] += (
                        far_ret[g, t, some(r), :].astype(jnp.float32)
                    )

            factor = scale if t == 0 else 1.0
            fin[g, t, some(r), :] = (owed(g, 0, t, r) * factor).astype(jnp.bfloat16)
            to_mate(g, t, r).start()

    for d in range(1, reach + 1):
        @pl.when(rank < d)
        def _(d=d):
            for g in range(kv_count):
                kt[g, :, slot(d)] = jnp.zeros((HEAD_SIZE, rows), jnp.bfloat16)
                stats[g, d, 0] = jnp.full((units, 2 * HALF), NEG, jnp.float32)
                stats[g, d, 1] = jnp.zeros((units, 2 * HALF), jnp.float32)
                stats[g, d, 2] = jnp.zeros((units, 2 * HALF), jnp.float32)
            for h in range(halves):
                lo, hi = part(d, h)
                for g in range(kv_count):
                    dsv[g, h, lo:hi, :] = jnp.zeros(
                        (hi - lo, pairs * 2 * HALF), jnp.bfloat16
                    )

    last = kv_count - 1
    def ready(g, t):
        for copy in group_loads(g, t):
            copy.wait()

    seg_load.wait()
    make_bias(0)
    ready(0, 0)
    look_keys(0, 0)
    for d in range(1, reach):
        receive_seg(d)
    for d in range(1, reach):
        receive(0, d, 0)
        biased(d)
        look_keys(0, d)
    ready(0, 1)
    look_values(0, 0)
    for d in range(1, reach):
        receive(0, d, 1)
    if last > 0:
        for t in range(2):
            send_own(1, t)
    for d in range(1, reach):
        look_values(0, d)
    receive_seg(reach)
    biased(reach)
    for g in range(kv_count):
        more = g < last
        if more:
            ready(g + 1, 0)
            look_keys(g + 1, 0)
        if g > 0:
            send_rest(g - 1, (1,))
        receive(g, reach, 0)
        look_keys(g, reach)
        combine_keys(g)
        settle(g, reach, 1)
        send_first(g, reach, (1,))
        for d in range(reach - 1, 0, -1):
            settle(g, d, 1)
            if more:
                send_first(g, d, (1,))
        if g > 0:
            send_rest(g - 1, (0,))
        receive(g, reach, 1)
        look_values(g, reach)
        combine_values(g)
        settle(g, reach, 0)
        send_first(g, reach, (0,))
        for d in range(reach - 1, 0, -1):
            if not more:
                send_first(g, d, (1,))
            settle(g, d, 0)
            send_first(g, d, (0,))
        if more:
            for d in range(1, reach):
                receive(g + 1, d, 0)
                look_keys(g + 1, d)
            ready(g + 1, 1)
            look_values(g + 1, 0)
            for d in range(1, reach):
                receive(g + 1, d, 1)
            if g + 2 < kv_count:
                for t in range(2):
                    send_own(g + 2, t)
            for d in range(1, reach):
                look_values(g + 1, d)
        settle(g, 0, 1)
        settle(g, 0, 0)
    for g in range(kv_count):
        query_gradients(g)
    send_rest(last, (1,))
    send_rest(last, (0,))
    for g in range(last):
        finish(g, (1, 0))
    finish(last, (1,))
    finish(last, (0,))

    for g in range(kv_count):
        for t in range(2):
            for r in range(halves):
                to_mate(g, t, r).wait()
            if shared:
                other[g, t] = (
                    fin[g, t].astype(jnp.float32) + pfin[g, t].astype(jnp.float32)
                ).astype(jnp.bfloat16)
            else:
                other[g, t] = pfin[g, t]
    for d in range(reach):
        @pl.when(has_up & (rank >= d))
        def _(d=d):
            forward_seg(d).wait_send()
            for g in range(kv_count):
                for t in range(2):
                    for r in range(halves):
                        forward(t, g, d, r).wait_send()
    for d in range(1, reach + 1):
        for g in range(kv_count):
            for t in range(2):
                if far and d == 2:
                    @pl.when(goes_far(rank, g, t))
                    def _(g=g, t=t):
                        for r in range(halves):
                            back_far(g, t, r).wait_send()

                    @pl.when((rank >= d) & jnp.logical_not(goes_far(rank, g, t)))
                    def _(g=g, t=t, d=d):
                        for r in range(halves):
                            back(g, d, t, r).wait_send()
                else:
                    @pl.when(rank >= d)
                    def _(g=g, t=t, d=d):
                        for r in range(halves):
                            back(g, d, t, r).wait_send()


def place(kv_count, shared, dqv, fin, other, dq_hbm, dk_hbm, dv_hbm, sem):
    kv = lax.axis_index("kv")
    copies = [pltpu.make_async_copy(dqv, dq_hbm, sem.at[0])]
    parts = [(other, 0)] if shared else [(fin, kv * kv_count), (other, (1 - kv) * kv_count)]
    for source, base in parts:
        for g in range(kv_count):
            start = g * HEAD_SIZE
            if not shared:
                start = pl.multiple_of((base + g) * HEAD_SIZE, HEAD_SIZE)
            for t, ref in ((0, dk_hbm), (1, dv_hbm)):
                copies.append(
                    pltpu.make_async_copy(
                        source.at[g, t], ref.at[:, pl.ds(start, HEAD_SIZE)], sem.at[len(copies)]
                    )
                )
    for copy in copies:
        copy.start()
    for copy in copies:
        copy.wait()


def shards(queries, key_matrix, value_matrix, out_grad, segments):
    n = lax.axis_size("ctx")
    rows = queries.shape[0]
    head_count = queries.shape[1] // HEAD_SIZE
    group_width = QUERY_HEADS // KEY_VALUE_HEADS
    kv_count = max(head_count // group_width, 1)
    per_kv = head_count // kv_count
    kv_here = key_matrix.shape[1] // HEAD_SIZE
    shared = kv_here < kv_count * lax.axis_size("kv")
    reach = n // 2
    window = (reach + 1) * rows
    width = reach * rows + HALF
    halves = rows // HALF
    pairs = per_kv // 2
    bf16, f32 = jnp.bfloat16, jnp.float32
    dma = pltpu.SemaphoreType.DMA
    anywhere = pl.BlockSpec(memory_space=pltpu.HBM)
    inner = pltpu.VMEM
    dqv, fin, other = pl.pallas_call(
        functools.partial(kernel, n, reach, rows, per_kv, kv_count, shared),
        out_shape=(
            inner(queries.shape, bf16),
            inner((kv_count, 2, rows, HEAD_SIZE), bf16),
            inner((kv_count, 2, rows, HEAD_SIZE), bf16),
        ),
        in_specs=[anywhere] * 5,
        out_specs=(pl.BlockSpec(memory_space=pltpu.VMEM),) * 3,
        scratch_shapes=[
            pltpu.VMEM((head_count, rows, HEAD_SIZE), bf16),
            pltpu.VMEM((head_count, rows, HEAD_SIZE), bf16),
            pltpu.VMEM((kv_count, pairs, halves, width, 2 * HALF), f32),
            pltpu.VMEM((kv_count, pairs, halves, width, 2 * HALF), f32),
            pltpu.VMEM((kv_count, reach + 1, 3, pairs * halves, 2 * HALF), f32),
            pltpu.VMEM((kv_count, reach + 1, pairs * halves, 2 * HALF), f32),
            pltpu.VMEM((kv_count, pairs * halves, 2 * HALF), f32),
            pltpu.VMEM((halves, width, pairs * 2 * HALF), bf16),
            pltpu.VMEM((kv_count, halves, width, pairs * 2 * HALF), bf16),
            pltpu.VMEM((2, kv_count, window, HEAD_SIZE), bf16),
            pltpu.VMEM((reach + 1, 1, rows), jnp.int32),
            pltpu.VMEM((halves, width, HALF), f32),
            pltpu.VMEM((kv_count, HEAD_SIZE, window), bf16),
            pltpu.VMEM((kv_count, 2, window, HEAD_SIZE), f32),
            pltpu.VMEM((kv_count, reach, 2, rows, HEAD_SIZE), bf16),
            pltpu.VMEM((kv_count, reach, 2, rows, HEAD_SIZE), bf16),
            pltpu.VMEM((kv_count, 2, rows, HEAD_SIZE), bf16),
            pltpu.VMEM((kv_count, 2, rows, HEAD_SIZE), bf16),
            dma((1,)),
            dma((2, head_count)),
            dma((2, kv_count)),
            dma((reach + 1,)),
            dma((reach + 1,)),
            dma((2, kv_count, reach + 1, halves)),
            dma((2, kv_count, reach + 1, halves)),
            dma((kv_count, reach, 2, halves)),
            dma((kv_count, reach, 2, halves)),
            dma((kv_count, 2, halves)),
            dma((kv_count, 2, halves)),
            dma((kv_count, 2, halves)),
            dma((kv_count, 2, halves)),
        ],
        compiler_params=pltpu.CompilerParams(
            collective_id=0, has_side_effects=True, vmem_limit_bytes=56 * 1024 * 1024
        ),
    )(queries, key_matrix, value_matrix, out_grad, segments.reshape(1, rows))
    return pl.pallas_call(
        functools.partial(place, kv_count, shared),
        out_shape=(
            jax.ShapeDtypeStruct(queries.shape, bf16),
            jax.ShapeDtypeStruct(key_matrix.shape, bf16),
            jax.ShapeDtypeStruct(value_matrix.shape, bf16),
        ),
        in_specs=[pl.BlockSpec(memory_space=pltpu.VMEM)] * 3,
        out_specs=(anywhere,) * 3,
        scratch_shapes=[dma((1 + 4 * kv_count,))],
        compiler_params=pltpu.CompilerParams(vmem_limit_bytes=4 * 1024 * 1024),
    )(dqv, fin, other)


def solution(mesh):
    return jax.shard_map(
        shards,
        mesh=mesh,
        in_specs=(
            P(("groups", "ctx"), ("tp", "kv")),
            P(("groups", "ctx"), "tp"),
            P(("groups", "ctx"), "tp"),
            P(("groups", "ctx"), ("tp", "kv")),
            P(("groups", "ctx")),
        ),
        out_specs=(
            P(("groups", "ctx"), ("tp", "kv")),
            P(("groups", "ctx"), "tp"),
            P(("groups", "ctx"), "tp"),
        ),
        check_vma=False,
    )
```

```python
import functools
import jax
import jax.numpy as jnp
from jax import lax
from jax.experimental import pallas as pl
from jax.experimental.pallas import tpu as pltpu
from jax.sharding import PartitionSpec as P

QUERY_HEADS = 64
KEY_VALUE_HEADS = 8
HEAD_SIZE = 128
HALF = 128
CHUNK = 32
PIECE = 128
LOG2E = 1.4426950408889634
NEG = -1e30
MESH = pl.DeviceIdType.MESH
NT = (((1,), (1,)), ((), ()))


def kernel(
    n, reach, rows, per_kv, kv_count, shared,
    q_hbm, k_hbm, v_hbm, g_hbm, seg_hbm,
    dqv, fin, other,
    qv, gv, ev, dpv, stats, fac, deltas, pv, dsv, win, segwin, bias, kt, acc, sendb, ret, far_ret, pfin,
    seg_sem, load_sem, own_sem, seg_send, seg_recv, send_sem, recv_sem, back_send, back_recv,
    pair_send, pair_recv, far_back_send, far_back_recv,
):
    rank = lax.axis_index("ctx")
    kv = lax.axis_index("kv")
    up = lax.rem(rank + 1, n)
    down = lax.rem(rank + n - 1, n)
    mate = 1 - kv
    scale = HEAD_SIZE ** -0.5
    width = reach * rows + HALF
    halves = rows // HALF
    pairs = per_kv // 2
    first = 0 if shared else kv * kv_count

    def cols(base, g):
        if shared:
            return pl.ds(g * HEAD_SIZE, HEAD_SIZE)
        return pl.ds(pl.multiple_of((base + g) * HEAD_SIZE, HEAD_SIZE), HEAD_SIZE)

    def slot(d):
        return pl.ds((reach - d) * rows, rows)

    seg_load = pltpu.make_async_copy(seg_hbm, segwin.at[0], seg_sem.at[0])

    def own(t, g):
        ref = k_hbm if t == 0 else v_hbm
        return pltpu.make_async_copy(
            ref.at[:, cols(first, g)], win.at[t, g, slot(0)], own_sem.at[t, g]
        )

    def load(t, head):
        ref, to = ((q_hbm, qv), (g_hbm, gv))[t]
        return pltpu.make_async_copy(
            ref.at[:, pl.ds(head * HEAD_SIZE, HEAD_SIZE)], to.at[head], load_sem.at[t, head]
        )

    def group_loads(g, t):
        return [own(t, g)] + [load(t, i) for i in range(g * per_kv, (g + 1) * per_kv)]

    def some(r):
        return pl.ds(r * HALF, HALF)

    def forward(t, g, d, r):
        ref = k_hbm if t == 0 else v_hbm
        at = (reach - d) * rows + r * HALF
        src = ref.at[some(r), cols(first, g)] if d == 0 else win.at[t, g, pl.ds(at, HALF)]
        return pltpu.make_async_remote_copy(
            src_ref=src,
            dst_ref=win.at[t, g, pl.ds(at - rows, HALF)],
            send_sem=send_sem.at[t, g, d, r],
            recv_sem=recv_sem.at[t, g, d + 1, r],
            device_id={"ctx": up},
            device_id_type=MESH,
        )

    def forward_seg(d):
        return pltpu.make_async_remote_copy(
            src_ref=seg_hbm if d == 0 else segwin.at[d],
            dst_ref=segwin.at[d + 1],
            send_sem=seg_send.at[d],
            recv_sem=seg_recv.at[d + 1],
            device_id={"ctx": up},
            device_id_type=MESH,
        )

    bits = rows // PIECE

    def bit(r):
        return pl.ds(r * PIECE, PIECE)

    def pieces(kinds):
        return [(t, r) for t in kinds for r in range(bits)]

    def back(g, d, t, r):
        return pltpu.make_async_remote_copy(
            src_ref=sendb.at[g, d - 1, t, bit(r)],
            dst_ref=ret.at[g, d - 1, t, bit(r)],
            send_sem=back_send.at[g, d - 1, t, r],
            recv_sem=back_recv.at[g, d - 1, t, r],
            device_id={"ctx": down},
            device_id_type=MESH,
        )

    def back_far(g, t, r):
        return pltpu.make_async_remote_copy(
            src_ref=sendb.at[g, 1, t, bit(r)],
            dst_ref=far_ret.at[g, t, bit(r)],
            send_sem=far_back_send.at[g, t, r],
            recv_sem=far_back_recv.at[g, t, r],
            device_id={"ctx": lax.rem(rank + n - 2, n)},
            device_id_type=MESH,
        )

    far = reach > 1

    def goes_far(of, g, t):
        yes = of == 2
        if g == kv_count - 1 and t in ():
            yes = yes | (of == n - 1)
        return yes

    def owed(g, d, t, r):
        return acc[g, t, pl.ds((reach - d) * rows + r * PIECE, PIECE), :]

    def to_mate(g, t, r):
        return pltpu.make_async_remote_copy(
            src_ref=fin.at[g, t, bit(r)],
            dst_ref=pfin.at[g, t, bit(r)],
            send_sem=pair_send.at[g, t, r],
            recv_sem=pair_recv.at[g, t, r],
            device_id={"kv": mate},
            device_id_type=MESH,
        )

    has_up = rank < n - 1

    barrier = pltpu.get_barrier_semaphore()
    pl.semaphore_signal(barrier, inc=1, device_id={"kv": mate}, device_id_type=MESH)

    @pl.when(has_up)
    def _():
        pl.semaphore_signal(barrier, inc=1, device_id={"ctx": up}, device_id_type=MESH)

    @pl.when(rank > 0)
    def _():
        pl.semaphore_signal(barrier, inc=1, device_id={"ctx": down}, device_id_type=MESH)

    expected = 1 + jnp.where(has_up, 1, 0) + jnp.where(rank > 0, 1, 0)
    if far:
        @pl.when(rank == 0)
        def _():
            pl.semaphore_signal(
                barrier, inc=1, device_id={"ctx": lax.rem(rank + 2, n)}, device_id_type=MESH
            )

        expected = expected + jnp.where(rank == 2, 1, 0)
    seg_load.start()
    for g in range(kv_count):
        for t in range(2):
            for copy in group_loads(g, t):
                copy.start()

    pl.semaphore_wait(barrier, expected)

    @pl.when(has_up)
    def _():
        forward_seg(0).start()
        for t in range(2):
            for r in range(halves):
                forward(t, 0, 0, r).start()

    units = pairs * halves

    def receive_seg(d):
        @pl.when(rank >= d)
        def _():
            forward_seg(d - 1).wait_recv()

        if d < reach:
            @pl.when((rank >= d) & has_up)
            def _():
                forward_seg(d).start()

    def receive(g, d, t):
        for r in range(halves):
            @pl.when(rank >= d)
            def _(r=r):
                forward(t, g, d - 1, r).wait_recv()

            if d < reach:
                @pl.when((rank >= d) & has_up)
                def _(r=r):
                    forward(t, g, d, r).start()

    def send_own(g, t):
        @pl.when(has_up)
        def _():
            for r in range(halves):
                forward(t, g, 0, r).start()

    def part(d, h):
        start = (reach - d) * rows - h * HALF
        return max(start, 0), min(start + rows, width)

    def make_bias(d):
        column = jnp.broadcast_to(segwin[d].astype(jnp.float32), (HALF, rows)).T
        for h in range(halves):
            lo, hi = part(d, h)
            begin = lo + h * HALF - (reach - d) * rows
            seg_q = segwin[0, :, h * HALF:(h + 1) * HALF].astype(jnp.float32)
            keep = column[begin:begin + hi - lo] == seg_q
            if d == 0:
                key_at = lax.broadcasted_iota(jnp.int32, (hi - lo, HALF), 0)
                query_at = lax.broadcasted_iota(jnp.int32, (hi - lo, HALF), 1)
                keep = keep & (key_at + begin <= query_at + h * HALF)
            bias[h, lo:hi, :] = jnp.where(keep, 0.0, NEG)

    def biased(d):
        @pl.when(rank >= d)
        def _():
            make_bias(d)

    def pair(ref, g, h, p):
        head = g * per_kv + 2 * p
        return ref[head:head + 2, h * HALF:(h + 1) * HALF, :].reshape(2 * HALF, HEAD_SIZE)

    def stack(ref, g, h):
        return ref[g * per_kv:(g + 1) * per_kv, h * HALF:(h + 1) * HALF, :].reshape(
            per_kv * HALF, HEAD_SIZE
        )

    def key_products(g, d, p, h):
        lo, hi = part(d, h)
        span = slice(lo + h * HALF, hi + h * HALF)
        s = lax.dot_general(
            win[0, g, span, :], pair(qv, g, h, p), NT, preferred_element_type=jnp.float32
        )
        b = bias[h, lo:hi, :]
        s = s + jnp.concatenate([b, b], axis=1)
        ev[g, p, h, lo:hi, :] = s
        u = p * halves + h
        stats[g, d, 0, u:u + 1, :] = jnp.max(s, axis=0, keepdims=True)

    def exponentials(g, d, p, h):
        lo, hi = part(d, h)
        u = p * halves + h
        peak = stats[g, d, 0, u:u + 1, :]
        total = jnp.zeros((8, 2 * HALF), jnp.float32)
        for c in range(lo, hi, CHUNK):
            at = slice(c, c + CHUNK)
            e = jnp.exp2((ev[g, p, h, at, :] - peak) * (scale * LOG2E))
            ev[g, p, h, at, :] = e
            total = total + jnp.sum(e.reshape(-1, 8, 2 * HALF), axis=0)
        stats[g, d, 1, u:u + 1, :] = jnp.sum(total, axis=0, keepdims=True)

    def value_products(g, d, p, h):
        lo, hi = part(d, h)
        span = slice(lo + h * HALF, hi + h * HALF)
        u = p * halves + h
        dp = lax.dot_general(
            win[1, g, span, :], pair(gv, g, h, p), NT, preferred_element_type=jnp.float32
        )
        dpv[g, p, h, lo:hi, :] = dp
        stats[g, d, 2, u:u + 1, :] = jnp.sum(ev[g, p, h, lo:hi, :] * dp, axis=0, keepdims=True)

    todo = [(p, h) for p in range(pairs) for h in range(halves)]

    def look_keys(g, d):
        @pl.when(rank >= d)
        def _():
            key_products(g, d, *todo[0])
            for i, at in enumerate(todo):
                if i + 1 < len(todo):
                    key_products(g, d, *todo[i + 1])
                exponentials(g, d, *at)

    def look_values(g, d):
        @pl.when(rank >= d)
        def _():
            for at in todo:
                value_products(g, d, *at)

    def combine_keys(g):
        peak = stats[g, 0, 0]
        for d in range(1, reach + 1):
            peak = jnp.maximum(peak, stats[g, d, 0])
        total = jnp.zeros((units, 2 * HALF), jnp.float32)
        for d in range(reach + 1):
            f = jnp.exp2((stats[g, d, 0] - peak) * (scale * LOG2E))
            fac[g, d] = f
            total = total + f * stats[g, d, 1]
        inv = 1.0 / total
        for d in range(reach + 1):
            fac[g, d] = fac[g, d] * inv

    def combine_values(g):
        weighted = jnp.zeros((units, 2 * HALF), jnp.float32)
        for d in range(reach + 1):
            weighted = weighted + fac[g, d] * stats[g, d, 2]
        deltas[g] = weighted

    def settle(g, d, t):
        @pl.when(rank >= d)
        def _():
            order = list(range(halves)) if d > 0 else list(range(halves - 1, -1, -1))
            for i, h in enumerate(order):
                lo, hi = part(d, h)
                for p in range(pairs):
                    u = p * halves + h
                    f = fac[g, d, u:u + 1, :]
                    there = slice(p * 2 * HALF, (p + 1) * 2 * HALF)
                    for c in range(lo, hi, CHUNK):
                        at = slice(c, c + CHUNK)
                        pn = ev[g, p, h, at, :] * f
                        if t == 0:
                            delta = deltas[g, u:u + 1, :]
                            dsv[g, h, at, there] = (
                                pn * (dpv[g, p, h, at, :] - delta)
                            ).astype(jnp.bfloat16)
                        else:
                            pv[h, at, there] = pn.astype(jnp.bfloat16)
            for i, h in enumerate(order):
                lo, hi = part(d, h)
                span = slice(lo + h * HALF, hi + h * HALF)
                low, ref = ((dsv.at[g], qv), (pv, gv))[t]
                out = jnp.dot(
                    low[h, lo:hi, :], stack(ref, g, h), preferred_element_type=jnp.float32
                )
                if i > 0:
                    acc[g, t, span, :] += out
                else:
                    acc[g, t, span, :] = out

    def query_gradients(g):
        for d in range(reach + 1):
            @pl.when(rank >= d)
            def _(d=d):
                kt[g, :, slot(d)] = win[0, g, slot(d), :].T
        for h in range(halves):
            dqt = jnp.dot(
                kt[g, :, h * HALF:h * HALF + width], dsv[g, h], preferred_element_type=jnp.float32
            )
            dq = (dqt * scale).T.astype(jnp.bfloat16)
            for i in range(per_kv):
                at = (g * per_kv + i) * HEAD_SIZE
                dqv[h * HALF:(h + 1) * HALF, at:at + HEAD_SIZE] = dq[i * HALF:(i + 1) * HALF]

    def start_back(g, d, t, r):
        if far and d == 2:
            away = goes_far(rank, g, t)

            @pl.when(away)
            def _():
                back_far(g, t, r).start()

            @pl.when(jnp.logical_not(away))
            def _():
                back(g, d, t, r).start()
        else:
            back(g, d, t, r).start()

    def alone(g, d, t):
        if d == reach:
            return rank >= d
        yes = jnp.logical_not(has_up)
        if far and d == 1:
            yes = yes | goes_far(rank + 1, g, t)
        return (rank >= d) & yes

    def send_first(g, d, kinds):
        for t in kinds:
            @pl.when(alone(g, d, t))
            def _(t=t):
                for r in range(bits):
                    sendb[g, d - 1, t, bit(r), :] = owed(g, d, t, r).astype(jnp.bfloat16)
                for r in range(bits):
                    start_back(g, d, t, r)

    def send_rest(g, kinds):
        for d in range(reach - 1, 0, -1):
            for t in kinds:
                @pl.when((rank >= d) & jnp.logical_not(alone(g, d, t)))
                def _(d=d, t=t):
                    for r in range(bits):
                        back(g, d + 1, t, r).wait_recv()
                        sendb[g, d - 1, t, bit(r), :] = (
                            owed(g, d, t, r) + ret[g, d, t, bit(r), :].astype(jnp.float32)
                        ).astype(jnp.bfloat16)
                        start_back(g, d, t, r)

    def finish(g, kinds):
        for t, r in pieces(kinds):
            @pl.when(has_up)
            def _(t=t, r=r):
                back(g, 1, t, r).wait_recv()
                acc[g, t, pl.ds(reach * rows + r * PIECE, PIECE), :] += (
                    ret[g, 0, t, bit(r), :].astype(jnp.float32)
                )

            if far:
                @pl.when(goes_far(rank + 2, g, t))
                def _(t=t, r=r):
                    back_far(g, t, r).wait_recv()
                    acc[g, t, pl.ds(reach * rows + r * PIECE, PIECE), :] += (
                        far_ret[g, t, bit(r), :].astype(jnp.float32)
                    )

            factor = scale if t == 0 else 1.0
            fin[g, t, bit(r), :] = (owed(g, 0, t, r) * factor).astype(jnp.bfloat16)
            to_mate(g, t, r).start()

    for d in range(1, reach + 1):
        @pl.when(rank < d)
        def _(d=d):
            for g in range(kv_count):
                kt[g, :, slot(d)] = jnp.zeros((HEAD_SIZE, rows), jnp.bfloat16)
                stats[g, d, 0] = jnp.full((units, 2 * HALF), NEG, jnp.float32)
                stats[g, d, 1] = jnp.zeros((units, 2 * HALF), jnp.float32)
                stats[g, d, 2] = jnp.zeros((units, 2 * HALF), jnp.float32)
            for h in range(halves):
                lo, hi = part(d, h)
                for g in range(kv_count):
                    dsv[g, h, lo:hi, :] = jnp.zeros(
                        (hi - lo, pairs * 2 * HALF), jnp.bfloat16
                    )

    last = kv_count - 1
    def ready(g, t):
        for copy in group_loads(g, t):
            copy.wait()

    seg_load.wait()
    make_bias(0)
    ready(0, 0)
    look_keys(0, 0)
    for d in range(1, reach):
        receive_seg(d)
    for d in range(1, reach):
        receive(0, d, 0)
        biased(d)
        look_keys(0, d)
    ready(0, 1)
    look_values(0, 0)
    for d in range(1, reach):
        receive(0, d, 1)
    if last > 0:
        for t in range(2):
            send_own(1, t)
    for d in range(1, reach):
        look_values(0, d)
    receive_seg(reach)
    biased(reach)
    for g in range(kv_count):
        more = g < last
        if more:
            ready(g + 1, 0)
            look_keys(g + 1, 0)
        if g > 0:
            send_rest(g - 1, (1,))
        receive(g, reach, 0)
        look_keys(g, reach)
        combine_keys(g)
        settle(g, reach, 1)
        send_first(g, reach, (1,))
        if more:
            for d in range(reach - 1, 0, -1):
                settle(g, d, 1)
                send_first(g, d, (1,))
        if g > 0:
            send_rest(g - 1, (0,))
        receive(g, reach, 1)
        look_values(g, reach)
        combine_values(g)
        settle(g, reach, 0)
        send_first(g, reach, (0,))
        for d in range(reach - 1, 0, -1):
            if not more:
                settle(g, d, 1)
                send_first(g, d, (1,))
            settle(g, d, 0)
            send_first(g, d, (0,))
        if more:
            for d in range(1, reach):
                receive(g + 1, d, 0)
                look_keys(g + 1, d)
            ready(g + 1, 1)
            look_values(g + 1, 0)
            for d in range(1, reach):
                receive(g + 1, d, 1)
            if g + 2 < kv_count:
                for t in range(2):
                    send_own(g + 2, t)
            for d in range(1, reach):
                look_values(g + 1, d)
    for g in range(last):
        settle(g, 0, 1)
        settle(g, 0, 0)
        query_gradients(g)
    send_rest(last, (1,))
    settle(last, 0, 1)
    settle(last, 0, 0)
    send_rest(last, (0,))
    query_gradients(last)
    for d in range(reach):
        @pl.when(has_up & (rank >= d))
        def _(d=d):
            forward_seg(d).wait_send()
            for g in range(kv_count):
                for t in range(2):
                    for r in range(halves):
                        forward(t, g, d, r).wait_send()
    for g in range(last):
        finish(g, (1, 0))
    finish(last, (1,))
    finish(last, (0,))

    for g in range(kv_count):
        for t in range(2):
            for r in range(bits):
                to_mate(g, t, r).wait()
            if shared:
                other[g, t] = (
                    fin[g, t].astype(jnp.float32) + pfin[g, t].astype(jnp.float32)
                ).astype(jnp.bfloat16)
            else:
                other[g, t] = pfin[g, t]
    for d in range(1, reach + 1):
        for g in range(kv_count):
            for t in range(2):
                if far and d == 2:
                    @pl.when(goes_far(rank, g, t))
                    def _(g=g, t=t):
                        for r in range(bits):
                            back_far(g, t, r).wait_send()

                    @pl.when((rank >= d) & jnp.logical_not(goes_far(rank, g, t)))
                    def _(g=g, t=t, d=d):
                        for r in range(bits):
                            back(g, d, t, r).wait_send()
                else:
                    @pl.when(rank >= d)
                    def _(g=g, t=t, d=d):
                        for r in range(bits):
                            back(g, d, t, r).wait_send()


def place(kv_count, shared, dqv, fin, other, dq_hbm, dk_hbm, dv_hbm, sem):
    kv = lax.axis_index("kv")
    copies = [pltpu.make_async_copy(dqv, dq_hbm, sem.at[0])]
    parts = [(other, 0)] if shared else [(fin, kv * kv_count), (other, (1 - kv) * kv_count)]
    for source, base in parts:
        for g in range(kv_count):
            start = g * HEAD_SIZE
            if not shared:
                start = pl.multiple_of((base + g) * HEAD_SIZE, HEAD_SIZE)
            for t, ref in ((0, dk_hbm), (1, dv_hbm)):
                copies.append(
                    pltpu.make_async_copy(
                        source.at[g, t], ref.at[:, pl.ds(start, HEAD_SIZE)], sem.at[len(copies)]
                    )
                )
    for copy in copies:
        copy.start()
    for copy in copies:
        copy.wait()


def shards(queries, key_matrix, value_matrix, out_grad, segments):
    n = lax.axis_size("ctx")
    rows = queries.shape[0]
    head_count = queries.shape[1] // HEAD_SIZE
    group_width = QUERY_HEADS // KEY_VALUE_HEADS
    kv_count = max(head_count // group_width, 1)
    per_kv = head_count // kv_count
    kv_here = key_matrix.shape[1] // HEAD_SIZE
    shared = kv_here < kv_count * lax.axis_size("kv")
    reach = n // 2
    window = (reach + 1) * rows
    width = reach * rows + HALF
    halves = rows // HALF
    pairs = per_kv // 2
    bf16, f32 = jnp.bfloat16, jnp.float32
    dma = pltpu.SemaphoreType.DMA
    anywhere = pl.BlockSpec(memory_space=pltpu.HBM)
    inner = pltpu.VMEM
    dqv, fin, other = pl.pallas_call(
        functools.partial(kernel, n, reach, rows, per_kv, kv_count, shared),
        out_shape=(
            inner(queries.shape, bf16),
            inner((kv_count, 2, rows, HEAD_SIZE), bf16),
            inner((kv_count, 2, rows, HEAD_SIZE), bf16),
        ),
        in_specs=[anywhere] * 5,
        out_specs=(pl.BlockSpec(memory_space=pltpu.VMEM),) * 3,
        scratch_shapes=[
            pltpu.VMEM((head_count, rows, HEAD_SIZE), bf16),
            pltpu.VMEM((head_count, rows, HEAD_SIZE), bf16),
            pltpu.VMEM((kv_count, pairs, halves, width, 2 * HALF), f32),
            pltpu.VMEM((kv_count, pairs, halves, width, 2 * HALF), f32),
            pltpu.VMEM((kv_count, reach + 1, 3, pairs * halves, 2 * HALF), f32),
            pltpu.VMEM((kv_count, reach + 1, pairs * halves, 2 * HALF), f32),
            pltpu.VMEM((kv_count, pairs * halves, 2 * HALF), f32),
            pltpu.VMEM((halves, width, pairs * 2 * HALF), bf16),
            pltpu.VMEM((kv_count, halves, width, pairs * 2 * HALF), bf16),
            pltpu.VMEM((2, kv_count, window, HEAD_SIZE), bf16),
            pltpu.VMEM((reach + 1, 1, rows), jnp.int32),
            pltpu.VMEM((halves, width, HALF), f32),
            pltpu.VMEM((kv_count, HEAD_SIZE, window), bf16),
            pltpu.VMEM((kv_count, 2, window, HEAD_SIZE), f32),
            pltpu.VMEM((kv_count, reach, 2, rows, HEAD_SIZE), bf16),
            pltpu.VMEM((kv_count, reach, 2, rows, HEAD_SIZE), bf16),
            pltpu.VMEM((kv_count, 2, rows, HEAD_SIZE), bf16),
            pltpu.VMEM((kv_count, 2, rows, HEAD_SIZE), bf16),
            dma((1,)),
            dma((2, head_count)),
            dma((2, kv_count)),
            dma((reach + 1,)),
            dma((reach + 1,)),
            dma((2, kv_count, reach + 1, halves)),
            dma((2, kv_count, reach + 1, halves)),
            dma((kv_count, reach, 2, rows // PIECE)),
            dma((kv_count, reach, 2, rows // PIECE)),
            dma((kv_count, 2, rows // PIECE)),
            dma((kv_count, 2, rows // PIECE)),
            dma((kv_count, 2, rows // PIECE)),
            dma((kv_count, 2, rows // PIECE)),
        ],
        compiler_params=pltpu.CompilerParams(
            collective_id=0, has_side_effects=True, vmem_limit_bytes=56 * 1024 * 1024
        ),
    )(queries, key_matrix, value_matrix, out_grad, segments.reshape(1, rows))
    return pl.pallas_call(
        functools.partial(place, kv_count, shared),
        out_shape=(
            jax.ShapeDtypeStruct(queries.shape, bf16),
            jax.ShapeDtypeStruct(key_matrix.shape, bf16),
            jax.ShapeDtypeStruct(value_matrix.shape, bf16),
        ),
        in_specs=[pl.BlockSpec(memory_space=pltpu.VMEM)] * 3,
        out_specs=(anywhere,) * 3,
        scratch_shapes=[dma((1 + 4 * kv_count,))],
        compiler_params=pltpu.CompilerParams(vmem_limit_bytes=4 * 1024 * 1024),
    )(dqv, fin, other)


def solution(mesh):
    return jax.shard_map(
        shards,
        mesh=mesh,
        in_specs=(
            P(("groups", "ctx"), ("tp", "kv")),
            P(("groups", "ctx"), "tp"),
            P(("groups", "ctx"), "tp"),
            P(("groups", "ctx"), ("tp", "kv")),
            P(("groups", "ctx")),
        ),
        out_specs=(
            P(("groups", "ctx"), ("tp", "kv")),
            P(("groups", "ctx"), "tp"),
            P(("groups", "ctx"), "tp"),
        ),
        check_vma=False,
    )
```

```python
import functools
import jax
import jax.numpy as jnp
from jax import lax
from jax.experimental import pallas as pl
from jax.experimental.pallas import tpu as pltpu
from jax.sharding import PartitionSpec as P

QUERY_HEADS = 64
KEY_VALUE_HEADS = 8
HEAD_SIZE = 128
HALF = 128
CHUNK = 32
PIECE = 128
LOG2E = 1.4426950408889634
NEG = -1e30
MESH = pl.DeviceIdType.MESH
NT = (((1,), (1,)), ((), ()))


def kernel(
    n, reach, rows, per_kv, kv_count, shared,
    q_hbm, k_hbm, v_hbm, g_hbm, seg_hbm,
    dqv, fin, other,
    qv, gv, ev, dpv, stats, fac, deltas, pv, dsv, win, segwin, bias, kt, acc, sendb, ret, far_ret, pfin,
    seg_sem, load_sem, own_sem, seg_send, seg_recv, send_sem, recv_sem, back_send, back_recv,
    pair_send, pair_recv, far_back_send, far_back_recv,
):
    rank = lax.axis_index("ctx")
    kv = lax.axis_index("kv")
    up = lax.rem(rank + 1, n)
    down = lax.rem(rank + n - 1, n)
    mate = 1 - kv
    scale = HEAD_SIZE ** -0.5
    width = reach * rows + HALF
    halves = rows // HALF
    pairs = per_kv // 2
    first = 0 if shared else kv * kv_count

    def cols(base, g):
        if shared:
            return pl.ds(g * HEAD_SIZE, HEAD_SIZE)
        return pl.ds(pl.multiple_of((base + g) * HEAD_SIZE, HEAD_SIZE), HEAD_SIZE)

    def slot(d):
        return pl.ds((reach - d) * rows, rows)

    seg_load = pltpu.make_async_copy(seg_hbm, segwin.at[0], seg_sem.at[0])

    def own(t, g):
        ref = k_hbm if t == 0 else v_hbm
        return pltpu.make_async_copy(
            ref.at[:, cols(first, g)], win.at[t, g, slot(0)], own_sem.at[t, g]
        )

    def load(t, head):
        ref, to = ((q_hbm, qv), (g_hbm, gv))[t]
        return pltpu.make_async_copy(
            ref.at[:, pl.ds(head * HEAD_SIZE, HEAD_SIZE)], to.at[head], load_sem.at[t, head]
        )

    def group_loads(g, t):
        return [own(t, g)] + [load(t, i) for i in range(g * per_kv, (g + 1) * per_kv)]

    def some(r):
        return pl.ds(r * HALF, HALF)

    def forward(t, g, d, r):
        ref = k_hbm if t == 0 else v_hbm
        at = (reach - d) * rows + r * HALF
        src = ref.at[some(r), cols(first, g)] if d == 0 else win.at[t, g, pl.ds(at, HALF)]
        return pltpu.make_async_remote_copy(
            src_ref=src,
            dst_ref=win.at[t, g, pl.ds(at - rows, HALF)],
            send_sem=send_sem.at[t, g, d, r],
            recv_sem=recv_sem.at[t, g, d + 1, r],
            device_id={"ctx": up},
            device_id_type=MESH,
        )

    def forward_seg(d):
        return pltpu.make_async_remote_copy(
            src_ref=seg_hbm if d == 0 else segwin.at[d],
            dst_ref=segwin.at[d + 1],
            send_sem=seg_send.at[d],
            recv_sem=seg_recv.at[d + 1],
            device_id={"ctx": up},
            device_id_type=MESH,
        )

    bits = rows // PIECE

    def bit(r):
        return pl.ds(r * PIECE, PIECE)

    def pieces(kinds):
        return [(t, r) for t in kinds for r in range(bits)]

    def back(g, d, t, r):
        return pltpu.make_async_remote_copy(
            src_ref=sendb.at[g, d - 1, t, bit(r)],
            dst_ref=ret.at[g, d - 1, t, bit(r)],
            send_sem=back_send.at[g, d - 1, t, r],
            recv_sem=back_recv.at[g, d - 1, t, r],
            device_id={"ctx": down},
            device_id_type=MESH,
        )

    def back_far(g, t, r):
        return pltpu.make_async_remote_copy(
            src_ref=sendb.at[g, 1, t, bit(r)],
            dst_ref=far_ret.at[g, t, bit(r)],
            send_sem=far_back_send.at[g, t, r],
            recv_sem=far_back_recv.at[g, t, r],
            device_id={"ctx": lax.rem(rank + n - 2, n)},
            device_id_type=MESH,
        )

    far = reach > 1

    def goes_far(of, g, t):
        yes = of == 2
        if g == kv_count - 1 and t in ():
            yes = yes | (of == n - 1)
        return yes

    def owed(g, d, t, r):
        return acc[g, t, pl.ds((reach - d) * rows + r * PIECE, PIECE), :]

    def to_mate(g, t, r):
        return pltpu.make_async_remote_copy(
            src_ref=fin.at[g, t, bit(r)],
            dst_ref=pfin.at[g, t, bit(r)],
            send_sem=pair_send.at[g, t, r],
            recv_sem=pair_recv.at[g, t, r],
            device_id={"kv": mate},
            device_id_type=MESH,
        )

    has_up = rank < n - 1

    barrier = pltpu.get_barrier_semaphore()
    pl.semaphore_signal(barrier, inc=1, device_id={"kv": mate}, device_id_type=MESH)

    @pl.when(has_up)
    def _():
        pl.semaphore_signal(barrier, inc=1, device_id={"ctx": up}, device_id_type=MESH)

    @pl.when(rank > 0)
    def _():
        pl.semaphore_signal(barrier, inc=1, device_id={"ctx": down}, device_id_type=MESH)

    expected = 1 + jnp.where(has_up, 1, 0) + jnp.where(rank > 0, 1, 0)
    if far:
        @pl.when(rank == 0)
        def _():
            pl.semaphore_signal(
                barrier, inc=1, device_id={"ctx": lax.rem(rank + 2, n)}, device_id_type=MESH
            )

        expected = expected + jnp.where(rank == 2, 1, 0)
    seg_load.start()
    for g in range(kv_count):
        for t in range(2):
            for copy in group_loads(g, t):
                copy.start()

    pl.semaphore_wait(barrier, expected)

    @pl.when(has_up)
    def _():
        forward_seg(0).start()
        for t in range(2):
            for r in range(halves):
                forward(t, 0, 0, r).start()

    units = pairs * halves

    def receive_seg(d):
        @pl.when(rank >= d)
        def _():
            forward_seg(d - 1).wait_recv()

        if d < reach:
            @pl.when((rank >= d) & has_up)
            def _():
                forward_seg(d).start()

    def receive(g, d, t):
        for r in range(halves):
            @pl.when(rank >= d)
            def _(r=r):
                forward(t, g, d - 1, r).wait_recv()

            if d < reach:
                @pl.when((rank >= d) & has_up)
                def _(r=r):
                    forward(t, g, d, r).start()

    def send_own(g, t):
        @pl.when(has_up)
        def _():
            for r in range(halves):
                forward(t, g, 0, r).start()

    def part(d, h):
        start = (reach - d) * rows - h * HALF
        return max(start, 0), min(start + rows, width)

    def make_bias(d):
        column = jnp.broadcast_to(segwin[d].astype(jnp.float32), (HALF, rows)).T
        for h in range(halves):
            lo, hi = part(d, h)
            begin = lo + h * HALF - (reach - d) * rows
            seg_q = segwin[0, :, h * HALF:(h + 1) * HALF].astype(jnp.float32)
            keep = column[begin:begin + hi - lo] == seg_q
            if d == 0:
                key_at = lax.broadcasted_iota(jnp.int32, (hi - lo, HALF), 0)
                query_at = lax.broadcasted_iota(jnp.int32, (hi - lo, HALF), 1)
                keep = keep & (key_at + begin <= query_at + h * HALF)
            bias[h, lo:hi, :] = jnp.where(keep, 0.0, NEG)

    def biased(d):
        @pl.when(rank >= d)
        def _():
            make_bias(d)

    def pair(ref, g, h, p):
        head = g * per_kv + 2 * p
        return ref[head:head + 2, h * HALF:(h + 1) * HALF, :].reshape(2 * HALF, HEAD_SIZE)

    def stack(ref, g, h):
        return ref[g * per_kv:(g + 1) * per_kv, h * HALF:(h + 1) * HALF, :].reshape(
            per_kv * HALF, HEAD_SIZE
        )

    def key_products(g, d, p, h):
        lo, hi = part(d, h)
        span = slice(lo + h * HALF, hi + h * HALF)
        s = lax.dot_general(
            win[0, g, span, :], pair(qv, g, h, p), NT, preferred_element_type=jnp.float32
        )
        b = bias[h, lo:hi, :]
        s = s + jnp.concatenate([b, b], axis=1)
        ev[g, p, h, lo:hi, :] = s
        u = p * halves + h
        stats[g, d, 0, u:u + 1, :] = jnp.max(s, axis=0, keepdims=True)

    def exponentials(g, d, p, h):
        lo, hi = part(d, h)
        u = p * halves + h
        peak = stats[g, d, 0, u:u + 1, :]
        total = jnp.zeros((8, 2 * HALF), jnp.float32)
        for c in range(lo, hi, CHUNK):
            at = slice(c, c + CHUNK)
            e = jnp.exp2((ev[g, p, h, at, :] - peak) * (scale * LOG2E))
            ev[g, p, h, at, :] = e
            total = total + jnp.sum(e.reshape(-1, 8, 2 * HALF), axis=0)
        stats[g, d, 1, u:u + 1, :] = jnp.sum(total, axis=0, keepdims=True)

    def value_products(g, d, p, h):
        lo, hi = part(d, h)
        span = slice(lo + h * HALF, hi + h * HALF)
        u = p * halves + h
        dp = lax.dot_general(
            win[1, g, span, :], pair(gv, g, h, p), NT, preferred_element_type=jnp.float32
        )
        dpv[g, p, h, lo:hi, :] = dp
        stats[g, d, 2, u:u + 1, :] = jnp.sum(ev[g, p, h, lo:hi, :] * dp, axis=0, keepdims=True)

    todo = [(p, h) for p in range(pairs) for h in range(halves)]

    def look_keys(g, d):
        @pl.when(rank >= d)
        def _():
            key_products(g, d, *todo[0])
            for i, at in enumerate(todo):
                if i + 1 < len(todo):
                    key_products(g, d, *todo[i + 1])
                exponentials(g, d, *at)

    def look_values(g, d):
        @pl.when(rank >= d)
        def _():
            for at in todo:
                value_products(g, d, *at)

    def combine_keys(g):
        peak = stats[g, 0, 0]
        for d in range(1, reach + 1):
            peak = jnp.maximum(peak, stats[g, d, 0])
        total = jnp.zeros((units, 2 * HALF), jnp.float32)
        for d in range(reach + 1):
            f = jnp.exp2((stats[g, d, 0] - peak) * (scale * LOG2E))
            fac[g, d] = f
            total = total + f * stats[g, d, 1]
        inv = 1.0 / total
        for d in range(reach + 1):
            fac[g, d] = fac[g, d] * inv

    def combine_values(g):
        weighted = jnp.zeros((units, 2 * HALF), jnp.float32)
        for d in range(reach + 1):
            weighted = weighted + fac[g, d] * stats[g, d, 2]
        deltas[g] = weighted

    def settle(g, d, t):
        @pl.when(rank >= d)
        def _():
            order = list(range(halves)) if d > 0 else list(range(halves - 1, -1, -1))
            for i, h in enumerate(order):
                lo, hi = part(d, h)
                for p in range(pairs):
                    u = p * halves + h
                    f = fac[g, d, u:u + 1, :]
                    there = slice(p * 2 * HALF, (p + 1) * 2 * HALF)
                    for c in range(lo, hi, CHUNK):
                        at = slice(c, c + CHUNK)
                        pn = ev[g, p, h, at, :] * f
                        if t == 0:
                            delta = deltas[g, u:u + 1, :]
                            dsv[g, h, at, there] = (
                                pn * (dpv[g, p, h, at, :] - delta)
                            ).astype(jnp.bfloat16)
                        else:
                            pv[h, at, there] = pn.astype(jnp.bfloat16)
            for i, h in enumerate(order):
                lo, hi = part(d, h)
                span = slice(lo + h * HALF, hi + h * HALF)
                low, ref = ((dsv.at[g], qv), (pv, gv))[t]
                out = jnp.dot(
                    low[h, lo:hi, :], stack(ref, g, h), preferred_element_type=jnp.float32
                )
                if i > 0:
                    acc[g, t, span, :] += out
                else:
                    acc[g, t, span, :] = out

    def query_gradients(g):
        for d in range(reach + 1):
            @pl.when(rank >= d)
            def _(d=d):
                kt[g, :, slot(d)] = win[0, g, slot(d), :].T
        for h in range(halves):
            dqt = jnp.dot(
                kt[g, :, h * HALF:h * HALF + width], dsv[g, h], preferred_element_type=jnp.float32
            )
            dq = (dqt * scale).T.astype(jnp.bfloat16)
            for i in range(per_kv):
                at = (g * per_kv + i) * HEAD_SIZE
                dqv[h * HALF:(h + 1) * HALF, at:at + HEAD_SIZE] = dq[i * HALF:(i + 1) * HALF]

    def start_back(g, d, t, r):
        if far and d == 2:
            away = goes_far(rank, g, t)

            @pl.when(away)
            def _():
                back_far(g, t, r).start()

            @pl.when(jnp.logical_not(away))
            def _():
                back(g, d, t, r).start()
        else:
            back(g, d, t, r).start()

    def alone(g, d, t):
        if d == reach:
            return rank >= d
        yes = jnp.logical_not(has_up)
        if far and d == 1:
            yes = yes | goes_far(rank + 1, g, t)
        return (rank >= d) & yes

    def send_first(g, d, kinds):
        for t in kinds:
            @pl.when(alone(g, d, t))
            def _(t=t):
                for r in range(bits):
                    sendb[g, d - 1, t, bit(r), :] = owed(g, d, t, r).astype(jnp.bfloat16)
                for r in range(bits):
                    start_back(g, d, t, r)

    def send_rest(g, kinds):
        for d in range(reach - 1, 0, -1):
            for t in kinds:
                @pl.when((rank >= d) & jnp.logical_not(alone(g, d, t)))
                def _(d=d, t=t):
                    for r in range(bits):
                        back(g, d + 1, t, r).wait_recv()
                        sendb[g, d - 1, t, bit(r), :] = (
                            owed(g, d, t, r) + ret[g, d, t, bit(r), :].astype(jnp.float32)
                        ).astype(jnp.bfloat16)
                        start_back(g, d, t, r)

    def finish(g, kinds):
        for t, r in pieces(kinds):
            @pl.when(has_up)
            def _(t=t, r=r):
                back(g, 1, t, r).wait_recv()
                acc[g, t, pl.ds(reach * rows + r * PIECE, PIECE), :] += (
                    ret[g, 0, t, bit(r), :].astype(jnp.float32)
                )

            if far:
                @pl.when(goes_far(rank + 2, g, t))
                def _(t=t, r=r):
                    back_far(g, t, r).wait_recv()
                    acc[g, t, pl.ds(reach * rows + r * PIECE, PIECE), :] += (
                        far_ret[g, t, bit(r), :].astype(jnp.float32)
                    )

            factor = scale if t == 0 else 1.0
            fin[g, t, bit(r), :] = (owed(g, 0, t, r) * factor).astype(jnp.bfloat16)
            to_mate(g, t, r).start()

    for d in range(1, reach + 1):
        @pl.when(rank < d)
        def _(d=d):
            for g in range(kv_count):
                kt[g, :, slot(d)] = jnp.zeros((HEAD_SIZE, rows), jnp.bfloat16)
                stats[g, d, 0] = jnp.full((units, 2 * HALF), NEG, jnp.float32)
                stats[g, d, 1] = jnp.zeros((units, 2 * HALF), jnp.float32)
                stats[g, d, 2] = jnp.zeros((units, 2 * HALF), jnp.float32)
            for h in range(halves):
                lo, hi = part(d, h)
                for g in range(kv_count):
                    dsv[g, h, lo:hi, :] = jnp.zeros(
                        (hi - lo, pairs * 2 * HALF), jnp.bfloat16
                    )

    last = kv_count - 1
    def ready(g, t):
        for copy in group_loads(g, t):
            copy.wait()

    seg_load.wait()
    make_bias(0)
    ready(0, 0)
    look_keys(0, 0)
    for d in range(1, reach):
        receive_seg(d)
    for d in range(1, reach):
        receive(0, d, 0)
        biased(d)
        look_keys(0, d)
    ready(0, 1)
    look_values(0, 0)
    for d in range(1, reach):
        receive(0, d, 1)
    if last > 0:
        for t in range(2):
            send_own(1, t)
    for d in range(1, reach):
        look_values(0, d)
    receive_seg(reach)
    biased(reach)
    for g in range(kv_count):
        more = g < last
        if more:
            ready(g + 1, 0)
            look_keys(g + 1, 0)
        if g > 0:
            send_rest(g - 1, (1,))
        receive(g, reach, 0)
        look_keys(g, reach)
        combine_keys(g)
        settle(g, reach, 1)
        send_first(g, reach, (1,))
        if more:
            for d in range(reach - 1, 0, -1):
                settle(g, d, 1)
                send_first(g, d, (1,))
        receive(g, reach, 1)
        look_values(g, reach)
        combine_values(g)
        settle(g, reach, 0)
        send_first(g, reach, (0,))
        if g > 0:
            send_rest(g - 1, (0,))
        for d in range(reach - 1, 0, -1):
            if not more:
                settle(g, d, 1)
                send_first(g, d, (1,))
            settle(g, d, 0)
            send_first(g, d, (0,))
        if more:
            for d in range(1, reach):
                receive(g + 1, d, 0)
                look_keys(g + 1, d)
            ready(g + 1, 1)
            look_values(g + 1, 0)
            for d in range(1, reach):
                receive(g + 1, d, 1)
            if g + 2 < kv_count:
                for t in range(2):
                    send_own(g + 2, t)
            for d in range(1, reach):
                look_values(g + 1, d)
    for g in range(last):
        settle(g, 0, 1)
        settle(g, 0, 0)
        query_gradients(g)
    send_rest(last, (1,))
    settle(last, 0, 1)
    settle(last, 0, 0)
    send_rest(last, (0,))
    query_gradients(last)
    for d in range(reach):
        @pl.when(has_up & (rank >= d))
        def _(d=d):
            forward_seg(d).wait_send()
            for g in range(kv_count):
                for t in range(2):
                    for r in range(halves):
                        forward(t, g, d, r).wait_send()
    for g in range(last):
        finish(g, (1, 0))
    finish(last, (1,))
    finish(last, (0,))

    for g in range(kv_count):
        for t in range(2):
            for r in range(bits):
                to_mate(g, t, r).wait()
            if shared:
                other[g, t] = (
                    fin[g, t].astype(jnp.float32) + pfin[g, t].astype(jnp.float32)
                ).astype(jnp.bfloat16)
            else:
                other[g, t] = pfin[g, t]
    for d in range(1, reach + 1):
        for g in range(kv_count):
            for t in range(2):
                if far and d == 2:
                    @pl.when(goes_far(rank, g, t))
                    def _(g=g, t=t):
                        for r in range(bits):
                            back_far(g, t, r).wait_send()

                    @pl.when((rank >= d) & jnp.logical_not(goes_far(rank, g, t)))
                    def _(g=g, t=t, d=d):
                        for r in range(bits):
                            back(g, d, t, r).wait_send()
                else:
                    @pl.when(rank >= d)
                    def _(g=g, t=t, d=d):
                        for r in range(bits):
                            back(g, d, t, r).wait_send()


def place(kv_count, shared, dqv, fin, other, dq_hbm, dk_hbm, dv_hbm, sem):
    kv = lax.axis_index("kv")
    copies = [pltpu.make_async_copy(dqv, dq_hbm, sem.at[0])]
    parts = [(other, 0)] if shared else [(fin, kv * kv_count), (other, (1 - kv) * kv_count)]
    for source, base in parts:
        for g in range(kv_count):
            start = g * HEAD_SIZE
            if not shared:
                start = pl.multiple_of((base + g) * HEAD_SIZE, HEAD_SIZE)
            for t, ref in ((0, dk_hbm), (1, dv_hbm)):
                copies.append(
                    pltpu.make_async_copy(
                        source.at[g, t], ref.at[:, pl.ds(start, HEAD_SIZE)], sem.at[len(copies)]
                    )
                )
    for copy in copies:
        copy.start()
    for copy in copies:
        copy.wait()


def shards(queries, key_matrix, value_matrix, out_grad, segments):
    n = lax.axis_size("ctx")
    rows = queries.shape[0]
    head_count = queries.shape[1] // HEAD_SIZE
    group_width = QUERY_HEADS // KEY_VALUE_HEADS
    kv_count = max(head_count // group_width, 1)
    per_kv = head_count // kv_count
    kv_here = key_matrix.shape[1] // HEAD_SIZE
    shared = kv_here < kv_count * lax.axis_size("kv")
    reach = n // 2
    window = (reach + 1) * rows
    width = reach * rows + HALF
    halves = rows // HALF
    pairs = per_kv // 2
    bf16, f32 = jnp.bfloat16, jnp.float32
    dma = pltpu.SemaphoreType.DMA
    anywhere = pl.BlockSpec(memory_space=pltpu.HBM)
    inner = pltpu.VMEM
    dqv, fin, other = pl.pallas_call(
        functools.partial(kernel, n, reach, rows, per_kv, kv_count, shared),
        out_shape=(
            inner(queries.shape, bf16),
            inner((kv_count, 2, rows, HEAD_SIZE), bf16),
            inner((kv_count, 2, rows, HEAD_SIZE), bf16),
        ),
        in_specs=[anywhere] * 5,
        out_specs=(pl.BlockSpec(memory_space=pltpu.VMEM),) * 3,
        scratch_shapes=[
            pltpu.VMEM((head_count, rows, HEAD_SIZE), bf16),
            pltpu.VMEM((head_count, rows, HEAD_SIZE), bf16),
            pltpu.VMEM((kv_count, pairs, halves, width, 2 * HALF), f32),
            pltpu.VMEM((kv_count, pairs, halves, width, 2 * HALF), f32),
            pltpu.VMEM((kv_count, reach + 1, 3, pairs * halves, 2 * HALF), f32),
            pltpu.VMEM((kv_count, reach + 1, pairs * halves, 2 * HALF), f32),
            pltpu.VMEM((kv_count, pairs * halves, 2 * HALF), f32),
            pltpu.VMEM((halves, width, pairs * 2 * HALF), bf16),
            pltpu.VMEM((kv_count, halves, width, pairs * 2 * HALF), bf16),
            pltpu.VMEM((2, kv_count, window, HEAD_SIZE), bf16),
            pltpu.VMEM((reach + 1, 1, rows), jnp.int32),
            pltpu.VMEM((halves, width, HALF), f32),
            pltpu.VMEM((kv_count, HEAD_SIZE, window), bf16),
            pltpu.VMEM((kv_count, 2, window, HEAD_SIZE), f32),
            pltpu.VMEM((kv_count, reach, 2, rows, HEAD_SIZE), bf16),
            pltpu.VMEM((kv_count, reach, 2, rows, HEAD_SIZE), bf16),
            pltpu.VMEM((kv_count, 2, rows, HEAD_SIZE), bf16),
            pltpu.VMEM((kv_count, 2, rows, HEAD_SIZE), bf16),
            dma((1,)),
            dma((2, head_count)),
            dma((2, kv_count)),
            dma((reach + 1,)),
            dma((reach + 1,)),
            dma((2, kv_count, reach + 1, halves)),
            dma((2, kv_count, reach + 1, halves)),
            dma((kv_count, reach, 2, rows // PIECE)),
            dma((kv_count, reach, 2, rows // PIECE)),
            dma((kv_count, 2, rows // PIECE)),
            dma((kv_count, 2, rows // PIECE)),
            dma((kv_count, 2, rows // PIECE)),
            dma((kv_count, 2, rows // PIECE)),
        ],
        compiler_params=pltpu.CompilerParams(
            collective_id=0, has_side_effects=True, vmem_limit_bytes=56 * 1024 * 1024
        ),
    )(queries, key_matrix, value_matrix, out_grad, segments.reshape(1, rows))
    return pl.pallas_call(
        functools.partial(place, kv_count, shared),
        out_shape=(
            jax.ShapeDtypeStruct(queries.shape, bf16),
            jax.ShapeDtypeStruct(key_matrix.shape, bf16),
            jax.ShapeDtypeStruct(value_matrix.shape, bf16),
        ),
        in_specs=[pl.BlockSpec(memory_space=pltpu.VMEM)] * 3,
        out_specs=(anywhere,) * 3,
        scratch_shapes=[dma((1 + 4 * kv_count,))],
        compiler_params=pltpu.CompilerParams(vmem_limit_bytes=4 * 1024 * 1024),
    )(dqv, fin, other)


def solution(mesh):
    return jax.shard_map(
        shards,
        mesh=mesh,
        in_specs=(
            P(("groups", "ctx"), ("tp", "kv")),
            P(("groups", "ctx"), "tp"),
            P(("groups", "ctx"), "tp"),
            P(("groups", "ctx"), ("tp", "kv")),
            P(("groups", "ctx")),
        ),
        out_specs=(
            P(("groups", "ctx"), ("tp", "kv")),
            P(("groups", "ctx"), "tp"),
            P(("groups", "ctx"), "tp"),
        ),
        check_vma=False,
    )
```
